256 devices in a mesh: stream: 16 (over y_lo, z), span: 8 (over y_hi, x), rep: 2 (over core).
Axes of the slice: x: 4, y: 4 (y_hi: 2, y_lo: 2; y = y_hi * 2 + y_lo), z: 8, core: 2. Of those that a mesh axis runs over, the one named last changes fastest.
Arguments:
- node_state: bfloat16 [2, 16, 8, 384, 512], P('rep', 'stream', 'span'), may hold values from -6 to 6
- node_cot: bfloat16 [2, 16, 8, 384, 512], P('rep', 'stream', 'span'), may hold values from -6 to 6
- edge_w1: bfloat16 [1, 512, 512], replicated, may hold values from -0.25 to 0.25
- edge_b1: float32 [1, 512], replicated, may hold values from -3 to 3
- edge_w2: bfloat16 [1, 512, 512], replicated, may hold values from -0.25 to 0.25
- node_w1: bfloat16 [1, 1024, 512], replicated, may hold values from -0.1875 to 0.1875
- node_b1: float32 [1, 512], replicated, may hold values from -3 to 3
- node_w2: bfloat16 [1, 512, 512], replicated, may hold values from -0.25 to 0.25
- norm_gain: float32 [1, 512], replicated, may hold values from 0.5 to 1.5
- tile_dst: int32 [16, 8, 24], P('stream', 'span'), may hold values from 0 to 2
- tile_src: int32 [16, 8, 24], P('stream', 'span'), may hold values from 0 to 6, as said below
- tile_count: int32 [16, 8], P('stream', 'span'), may hold values from 6 to 24, as said below
- tile_vals: bfloat16 [16, 8, 24, 128, 128], P('stream', 'span'), may hold values from -0.29882812 to 0.29882812
- send_blocks: int32 [16, 8, 4, 1], P('stream', 'span'), may hold values from 0 to 2
Outputs:
- final_state: bfloat16 [2, 16, 8, 384, 512], P('rep', 'stream', 'span')
- state_grad: bfloat16 [2, 16, 8, 384, 512], P('rep', 'stream', 'span')
- edge_w1_grad: float32 [512, 512], P(('stream', 'span'))
- edge_w2_grad: float32 [512, 512], P(('stream', 'span'))
- node_w1_grad: float32 [1024, 512], P(('stream', 'span'))
- node_w2_grad: float32 [512, 512], P(('stream', 'span'))
The draws below stay inside these ranges and needn't reach their ends.
Inputs may be any that keep to these rules, and one draw needn't show every extreme that they name: `tile_src`: entries below 3 name own blocks, the others received ones; every received block is named by one of each partition's first 4 slots. `tile_count`: the live slots are the first ones; some partition uses all 24.
All inputs are finite; a program needn't handle non-finite values.
Results may differ from the reference program's by a relative error of at most 0.02.
Values may be sent and summed in bfloat16 or wider, within the bound.
A program may use at most 64 MiB of HBM per device.

```python
import jax
import jax.numpy as jnp
from jax import lax

H = 512
BLOCK = 128
NODES_DEV = 384
STEPS = 1
HALO_BLOCKS = 1
BLK = 3
TILES_DEV = 24
EXTENT = 7
STREAM_PARTS = 16
SPAN_PARTS = 8
SAMPLES = 2


def draw_tile_src(key, part):
    key_first = jax.random.fold_in(key, 11)
    key_rest = jax.random.fold_in(key, 12)
    group_total = 4 * HALO_BLOCKS
    rotation = jax.random.randint(key_first, (STREAM_PARTS, SPAN_PARTS, 1), 0, group_total)
    leading = BLK + (jnp.arange(group_total, dtype=jnp.int32)[None, None, :] + rotation) % group_total
    trailing = jax.random.randint(key_rest, (STREAM_PARTS, SPAN_PARTS, TILES_DEV - group_total), 0, EXTENT)
    return jnp.concatenate([leading.astype(jnp.int32), trailing.astype(jnp.int32)], axis=2)


def draw_tile_count(key, part):
    key_level = jax.random.fold_in(key, 21)
    key_chosen = jax.random.fold_in(key, 22)
    lowest = TILES_DEV // 4
    levels = jax.random.randint(key_level, (STREAM_PARTS, SPAN_PARTS), 0, 9)
    counts = lowest + (TILES_DEV - lowest) * levels * levels // 64
    chosen = jax.random.randint(key_chosen, (), 0, STREAM_PARTS * SPAN_PARTS)
    flat_counts = jnp.where(jnp.arange(STREAM_PARTS * SPAN_PARTS, dtype=jnp.int32) == chosen, TILES_DEV, counts.reshape(-1))
    return flat_counts.reshape(STREAM_PARTS, SPAN_PARTS).astype(jnp.int32)


def place_ends(array, own_key, least, largest):
    extent = array.shape
    place = [jax.random.randint(jax.random.fold_in(own_key, axis), (), 0, extent[axis]) for axis in range(len(extent))]
    array = array.at[tuple(place)].set(least)
    longest = extent.index(max(extent))
    place[longest] = (place[longest] + 1) % extent[longest]
    return array.at[tuple(place)].set(largest)


def block_levels(key, dims, cuts, low, high):
    gain, own = 1.0, jax.random.fold_in(key, 6)
    for dim, blocks in cuts:
        draws = jnp.exp(jax.random.uniform(jax.random.fold_in(own, dim), (blocks,), jnp.float32, low / len(cuts), high / len(cuts)))
        gain = gain * jnp.repeat(draws, dims[dim] // blocks).reshape([-1 if axis == dim else 1 for axis in range(len(dims))])
    return gain


def normal_values(key, extent, scale, most, split=(), held_as=jnp.bfloat16):
    loudness = block_levels(key, extent, split, -0.22, 0.18) if split else 1.0
    values = jax.random.normal(key, extent, jnp.float32) * scale * loudness
    return jnp.minimum(jnp.maximum(values, -most), most).astype(held_as)


def setup_inputs(seed: int = 0) -> dict:
    arg_keys = jax.random.split(jax.random.key(seed), 15)
    return {
        "node_state": normal_values(arg_keys[0], (SAMPLES, STREAM_PARTS, SPAN_PARTS, NODES_DEV, H), 1.0, 6.0, ((0, 2), (1, 16), (2, 8))),
        "node_cot": normal_values(arg_keys[1], (SAMPLES, STREAM_PARTS, SPAN_PARTS, NODES_DEV, H), 1.0, 6.0, ((0, 2), (1, 16), (2, 8))),
        "edge_w1": normal_values(arg_keys[2], (STEPS, H, H), H ** -0.5, 0.25),
        "edge_b1": normal_values(arg_keys[3], (STEPS, H), 0.5, 3.0, (), jnp.float32),
        "edge_w2": normal_values(arg_keys[4], (STEPS, H, H), H ** -0.5, 0.25),
        "node_w1": normal_values(arg_keys[5], (STEPS, 2 * H, H), (2 * H) ** -0.5, 0.1875),
        "node_b1": normal_values(arg_keys[6], (STEPS, H), 0.5, 3.0, (), jnp.float32),
        "node_w2": normal_values(arg_keys[7], (STEPS, H, H), H ** -0.5, 0.25),
        "norm_gain": jnp.clip(1.0 + 0.1 * jax.random.normal(arg_keys[8], (STEPS, H), jnp.float32), 0.5, 1.5),
        "tile_dst": place_ends(jax.random.randint(arg_keys[9], (STREAM_PARTS, SPAN_PARTS, TILES_DEV), 0, BLK), jax.random.fold_in(arg_keys[9], 1), 0, BLK - 1).astype(jnp.int32),
        "tile_src": draw_tile_src(jax.random.fold_in(arg_keys[14], 71), 0),
        "tile_count": draw_tile_count(jax.random.fold_in(arg_keys[14], 71), 0),
        "tile_vals": normal_values(arg_keys[12], (STREAM_PARTS, SPAN_PARTS, TILES_DEV, BLOCK, BLOCK), 0.05, 0.29882812, ((0, 16), (1, 8))),
        "send_blocks": place_ends(jax.random.randint(arg_keys[13], (STREAM_PARTS, SPAN_PARTS, 4, HALO_BLOCKS), 0, BLK), jax.random.fold_in(arg_keys[13], 1), 0, BLK - 1).astype(jnp.int32),
    }


norm_epsilon = 1e-05

def silu_slope(pre_value):
    logistic = jax.nn.sigmoid(pre_value)
    return logistic * (1.0 + pre_value * (1.0 - logistic))

def matmul(left_op, right_op):
    return jnp.dot(left_op, right_op, preferred_element_type=jnp.float32)

def edge_forward(state_rows, weight_in, bias_in, weight_out):
    pre_act = matmul(state_rows, weight_in) + bias_in
    hidden = jax.nn.silu(pre_act).astype(jnp.bfloat16)
    message = matmul(hidden, weight_out).astype(jnp.bfloat16)
    return (message, pre_act, hidden)

def node_forward(state_rows, gathered, weight_in, bias_in, weight_out, gain_vec):
    feature_width = state_rows.shape[1]
    pre_act = matmul(state_rows, weight_in[:feature_width]) + matmul(gathered, weight_in[feature_width:]) + bias_in
    hidden = jax.nn.silu(pre_act).astype(jnp.bfloat16)
    output = matmul(hidden, weight_out)
    centred = output - lax.optimization_barrier(jnp.mean(output, axis=1, keepdims=True))
    inverse_std = lax.rsqrt(lax.optimization_barrier(jnp.mean(centred * centred, axis=1, keepdims=True)) + norm_epsilon)
    normed = centred * inverse_std
    new_state = (state_rows.astype(jnp.float32) + normed * gain_vec).astype(jnp.bfloat16)
    return (new_state, pre_act, hidden, normed, inverse_std)

def edge_backward(state_rows, pre_act, hidden, weight_in, weight_out, cot_message):
    grad_out = jnp.dot(hidden.T, cot_message, preferred_element_type=jnp.float32)
    cot_hidden = jnp.dot(cot_message, weight_out.T, preferred_element_type=jnp.float32)
    cot_pre = (cot_hidden * silu_slope(pre_act)).astype(jnp.bfloat16)
    grad_in = jnp.dot(state_rows.T, cot_pre, preferred_element_type=jnp.float32)
    cot_state = jnp.dot(cot_pre, weight_in.T, preferred_element_type=jnp.float32)
    return (cot_state, grad_in, grad_out)

def node_backward(state_rows, gathered, pre_act, hidden, normed, inverse_std, weight_in, weight_out, gain_vec, cot_new):
    feature_width = state_rows.shape[1]
    carried = cot_new.astype(jnp.float32)
    scaled = carried * gain_vec
    cot_output = inverse_std * (scaled - lax.optimization_barrier(jnp.mean(scaled, axis=1, keepdims=True)) - normed * lax.optimization_barrier(jnp.mean(scaled * normed, axis=1, keepdims=True)))
    cot_output = cot_output.astype(jnp.bfloat16)
    grad_out = jnp.dot(hidden.T, cot_output, preferred_element_type=jnp.float32)
    cot_hidden = jnp.dot(cot_output, weight_out.T, preferred_element_type=jnp.float32)
    cot_pre = (cot_hidden * silu_slope(pre_act)).astype(jnp.bfloat16)
    grad_in = jnp.concatenate([jnp.dot(state_rows.T, cot_pre, preferred_element_type=jnp.float32), jnp.dot(gathered.T, cot_pre, preferred_element_type=jnp.float32)], axis=0)
    cot_gathered = jnp.dot(cot_pre, weight_in[feature_width:].T, preferred_element_type=jnp.float32).astype(jnp.bfloat16)
    cot_state = carried + jnp.dot(cot_pre, weight_in[:feature_width].T, preferred_element_type=jnp.float32)
    return (cot_state, cot_gathered, grad_in, grad_out)

def shift_down(tensor, along_axis):
    zero_rim = jnp.zeros_like(lax.slice_in_dim(tensor, 0, 1, axis=along_axis))
    kept = lax.slice_in_dim(tensor, 0, tensor.shape[along_axis] - 1, axis=along_axis)
    return jnp.concatenate([zero_rim, kept], axis=along_axis)

def shift_up(tensor, along_axis):
    zero_rim = jnp.zeros_like(lax.slice_in_dim(tensor, 0, 1, axis=along_axis))
    kept = lax.slice_in_dim(tensor, 1, tensor.shape[along_axis], axis=along_axis)
    return jnp.concatenate([kept, zero_rim], axis=along_axis)

def group_of(tensor, group_idx):
    return tensor[:, :, :, group_idx * HALO_BLOCKS:(group_idx + 1) * HALO_BLOCKS]

def assemble(message_blocks, select):
    as_float = message_blocks.astype(jnp.float32)
    sent = jnp.einsum('spjb,aspbch->aspjch', select, as_float)
    received = [shift_down(group_of(sent, 1), 1), shift_up(group_of(sent, 0), 1), shift_down(group_of(sent, 3), 2), shift_up(group_of(sent, 2), 2)]
    return jnp.concatenate([as_float] + received, axis=3).astype(jnp.bfloat16)

def fold_back(cot_extended, select):
    rounded = lax.optimization_barrier(cot_extended[:, :, :, BLK:].astype(jnp.bfloat16)).astype(jnp.float32)
    returned = jnp.concatenate([shift_down(group_of(rounded, 1), 1), shift_up(group_of(rounded, 0), 1), shift_down(group_of(rounded, 3), 2), shift_up(group_of(rounded, 2), 2)], axis=3)
    added_back = jnp.einsum('spjb,aspjch->aspbch', select, returned)
    return (cot_extended[:, :, :, :BLK] + added_back).astype(jnp.bfloat16)

def aggregate(extended, values, targets, sources, live_count):
    slot_count = values.shape[0]
    picked = jnp.take(extended, sources, axis=0).astype(jnp.float32)
    products = jnp.einsum('tab,tbh->tah', values.astype(jnp.float32), picked)
    live_mask = (jnp.arange(slot_count, dtype=jnp.int32) < live_count).astype(jnp.float32)
    select = (targets[:, None] == jnp.arange(BLK, dtype=jnp.int32)[None, :]).astype(jnp.float32) * live_mask[:, None]
    return jnp.einsum('tb,tah->bah', select, products).astype(jnp.bfloat16)

def spread(cot_blocks, values, targets, sources, live_count):
    slot_count = values.shape[0]
    picked = jnp.take(cot_blocks, targets, axis=0).astype(jnp.float32)
    products = jnp.einsum('tab,tah->tbh', values.astype(jnp.float32), picked)
    products = lax.optimization_barrier(products.astype(jnp.bfloat16)).astype(jnp.float32)
    live_mask = (jnp.arange(slot_count, dtype=jnp.int32) < live_count).astype(jnp.float32)
    select = (sources[:, None] == jnp.arange(EXTENT, dtype=jnp.int32)[None, :]).astype(jnp.float32) * live_mask[:, None]
    return jnp.einsum('te,tah->eah', select, products)

def over_devices(kernel, field, tile_vals, tile_dst, tile_src, tile_count):
    full_shape = field.shape
    parts = full_shape[1] * full_shape[2]
    by_device = jnp.moveaxis(field.reshape((full_shape[0], parts) + full_shape[3:]), 0, 1)

    def one_device(packed):
        field_part, values, targets, sources, live_count = packed
        return jax.vmap(kernel, in_axes=(0, None, None, None, None))(field_part, values, targets, sources, live_count)
    result = lax.map(one_device, (by_device, tile_vals.reshape((parts,) + tile_vals.shape[2:]), tile_dst.reshape(parts, -1), tile_src.reshape(parts, -1), tile_count.reshape(parts)))
    result = jnp.moveaxis(result, 1, 0)
    return result.reshape(full_shape[:3] + result.shape[2:])

def reference(node_state, node_cot, edge_w1, edge_b1, edge_w2, node_w1, node_b1, node_w2, norm_gain, tile_dst, tile_src, tile_count, tile_vals, send_blocks):
    lead_shape = node_state.shape[:3]
    feature_width = node_state.shape[4]
    block_shape = lead_shape + (BLK, BLOCK, feature_width)
    send_list = send_blocks.reshape(lead_shape[1], lead_shape[2], -1)
    select = (send_list[:, :, :, None] == jnp.arange(BLK, dtype=jnp.int32)).astype(jnp.float32)

    def layer_forward(state_rows, layer_idx):
        message, edge_pre, edge_hidden = edge_forward(state_rows, edge_w1[layer_idx], edge_b1[layer_idx], edge_w2[layer_idx])
        extended = assemble(message.reshape(block_shape), select)
        gathered = over_devices(aggregate, extended, tile_vals, tile_dst, tile_src, tile_count).reshape(-1, feature_width)
        node_parts = node_forward(state_rows, gathered, node_w1[layer_idx], node_b1[layer_idx], node_w2[layer_idx], norm_gain[layer_idx])
        return (edge_pre, edge_hidden, gathered) + node_parts
    states = [node_state.reshape(-1, feature_width)]
    for layer_idx in range(STEPS):
        states.append(layer_forward(states[-1], layer_idx)[3])
    cot_state = node_cot.reshape(-1, feature_width)
    grads_e1, grads_e2, grads_n1, grads_n2 = ([], [], [], [])
    for layer_idx in range(STEPS - 1, -1, -1):
        state_rows = states[layer_idx]
        edge_pre, edge_hidden, gathered, new_state, node_pre, node_hidden, normed, inverse_std = layer_forward(state_rows, layer_idx)
        cot_node_state, cot_gathered, grad_n1, grad_n2 = node_backward(state_rows, gathered, node_pre, node_hidden, normed, inverse_std, node_w1[layer_idx], node_w2[layer_idx], norm_gain[layer_idx], cot_state)
        cot_extended = over_devices(spread, cot_gathered.reshape(block_shape), tile_vals, tile_dst, tile_src, tile_count)
        cot_message = fold_back(cot_extended, select).reshape(-1, feature_width)
        cot_edge_state, grad_e1, grad_e2 = edge_backward(state_rows, edge_pre, edge_hidden, edge_w1[layer_idx], edge_w2[layer_idx], cot_message)
        cot_state = (cot_node_state + cot_edge_state).astype(jnp.bfloat16)
        grads_e1.insert(0, grad_e1)
        grads_e2.insert(0, grad_e2)
        grads_n1.insert(0, grad_n1)
        grads_n2.insert(0, grad_n2)
    final_state = states[-1].reshape(node_state.shape)
    state_grad = cot_state.reshape(node_state.shape)
    return (final_state, state_grad, jnp.concatenate(grads_e1, axis=0), jnp.concatenate(grads_e2, axis=0), jnp.concatenate(grads_n1, axis=0), jnp.concatenate(grads_n2, axis=0))
```

```python
import functools

import jax
import jax.numpy as jnp
from jax import lax
from jax.experimental import pallas as pl
from jax.experimental.pallas import tpu as pltpu
from jax.sharding import PartitionSpec as P

norm_epsilon = 1e-05
f32, bf16, i32 = jnp.float32, jnp.bfloat16, jnp.int32
MESH = pl.DeviceIdType.MESH
Y_LO = 2
Y_HI = 2
BLK = 3
EXTENT = 7


def log2(n):
    assert n & (n - 1) == 0
    return n.bit_length() - 1


def mm(left_op, right_op):
    return jnp.dot(left_op, right_op, preferred_element_type=f32)


def nt(left_op, right_op):
    return lax.dot_general(left_op, right_op, (((1,), (1,)), ((), ())), preferred_element_type=f32)


def loop(total, step, fn):
    def trip(i, carry):
        fn(pl.multiple_of(i * step, step))
        return carry

    lax.fori_loop(0, total // step, trip, 0)


def kernel(
    Z, X, H, B, T,
    dst_s, src_s, cnt_s, snd_s,
    eb1, nb1, gain,
    st_h, ct_h, ew1_h, ew2_h, nw1_h, nw2_h, vals_h,
    fs_h, sg_h, ge1, ge2, gn1, gn2,
    st, ct, ew1, ew2, nw1, nw2, vals, in_sem,
    slope, hid, msg, ext, sendb, mask, amat, amat_t, p4a, p4b, p8,
    he_t, s4_t, sg8_t, hn_t, part, gath, cot_out, cot_pre, cot_g, csp, own, tmp, tmp2, fsv,
    rets, ret, cot_msg, cot_pre_e,
    n_keep, n_r0s, n_r0, n_s1s, n_s1, n_s2s, n_s2, n_s3s, n_s3, n_fs, n_f,
    e_keep, e_r0s, e_r0, e_s1s, e_s1, e_s2s, e_s2, e_s3s, e_s3, e_fs, e_f,
    halo_ss, halo_rs, ret_ss, ret_rs, n_ss, n_rs, e_ss, e_rs, out_sem,
):
    R = BLK * B
    HC = H // 2
    Y = Y_LO * Y_HI
    SHARDS = Z * X * Y
    K4 = H // SHARDS
    s = lax.axis_index("stream")
    p = lax.axis_index("span")
    r = lax.axis_index("rep")
    y_lo, z = s // Z, s % Z
    y_hi, x = p // X, p % X
    y = y_hi * Y_LO + y_lo
    first = r == 0
    a = jnp.where(first, y, x)
    b = jnp.where(first, x, y)
    has = (s > 0, s < Y_LO * Z - 1, p > 0, p < Y_HI * X - 1)

    def at(yy, xx, zz):
        return {"stream": (yy % Y_LO) * Z + zz, "span": (yy // Y_LO) * X + xx, "rep": r}

    def a_peer(j):
        return at(jnp.where(first, (y + j) % Y, y), jnp.where(first, x, (x + j) % X), z)

    def b_peer(j):
        return at(jnp.where(first, y, (y + j) % Y), jnp.where(first, (x + j) % X, x), z)

    def z_peer(j):
        return at(y, x, (z + j) % Z)

    partner = {"stream": s, "span": p, "rep": 1 - r}
    sides = (
        {"stream": s - 1, "span": p, "rep": r},
        {"stream": s + 1, "span": p, "rep": r},
        {"stream": s, "span": p - 1, "rep": r},
        {"stream": s, "span": p + 1, "rep": r},
    )

    def remote(src, dst, ssem, rsem, dev):
        return pltpu.make_async_remote_copy(
            src_ref=src, dst_ref=dst, send_sem=ssem, recv_sem=rsem, device_id=dev, device_id_type=MESH
        )

    barrier = pltpu.get_barrier_semaphore()
    peers = [partner] + [a_peer(j) for j in range(1, 4)] + [b_peer(j) for j in range(1, 4)]
    peers += [z_peer(j) for j in range(1, Z)]
    for dev in peers:
        pl.semaphore_signal(barrier, inc=1, device_id=dev, device_id_type=MESH)
    halo_count = 0
    for side in range(4):
        halo_count = halo_count + has[side].astype(i32)

        @pl.when(has[side])
        def _():
            pl.semaphore_signal(barrier, inc=1, device_id=sides[side], device_id_type=MESH)

    loads = [
        pltpu.make_async_copy(src, dst, in_sem.at[i])
        for i, (src, dst) in enumerate(
            ((st_h, st), (ew1_h, ew1), (ew2_h, ew2), (vals_h, vals), (nw1_h, nw1), (nw2_h, nw2), (ct_h, ct))
        )
    ]
    for copy in loads:
        copy.start()

    CH = min(32, B)
    loads[0].wait()
    loads[1].wait()
    tmp[...] = mm(st[...], ew1[...])

    def edge_act(i):
        rows = pl.ds(i, CH)
        pre = tmp[rows, :] + eb1[...]
        g = jax.nn.sigmoid(pre)
        hid[rows, :] = (pre * g).astype(bf16)
        slope[rows, :] = g * (1.0 + pre * (1.0 - g))

    loop(R, CH, edge_act)
    loads[2].wait()
    tmp[...] = mm(hid[...], ew2[...])
    for blk in range(BLK):
        msg[blk] = tmp[blk * B : (blk + 1) * B, :].astype(bf16)
    for j in range(4):
        sendb[j] = msg[snd_s[j]]
    pl.semaphore_wait(barrier, len(peers) + halo_count)

    back = (1, 0, 3, 2)
    halo = [
        remote(sendb.at[j], ext.at[back[j]], halo_ss.at[j], halo_rs.at[back[j]], sides[j]) for j in range(4)
    ]
    for j in range(4):

        @pl.when(has[j])
        def _():
            halo[j].start()

        @pl.when(jnp.logical_not(has[j]))
        def _():
            ext[j] = jnp.zeros((B, H), bf16)
            ret[j] = jnp.zeros((B, H), bf16)

    def masks(t, carry):
        key = jnp.where(t < cnt_s[0], dst_s[t] * EXTENT + src_s[t], -1)
        keys = jnp.full((8, B), key, i32)
        for q in range(BLK * EXTENT):
            mask[t, q] = jnp.where(keys == q, 1.0, 0.0).astype(f32)
        return carry

    lax.fori_loop(0, T, masks, 0)
    loads[3].wait()

    def tiles(i):
        totals = [[jnp.zeros((8, B), f32)] * 2 for _ in range(BLK * EXTENT)]
        for t in range(T):
            v = vals[t, pl.ds(i, 16), :].astype(f32)
            halves = (v[:8], v[8:])
            for q in range(BLK * EXTENT):
                m = mask[t, q]
                totals[q] = [totals[q][0] + m * halves[0], totals[q][1] + m * halves[1]]
        for q in range(BLK * EXTENT):
            d, e = q // EXTENT, q % EXTENT
            amat[pl.ds(pl.multiple_of(d * B + i, 16), 16), e * B : (e + 1) * B] = jnp.concatenate(
                totals[q], axis=0
            ).astype(bf16)

    loop(B, 16, tiles)
    eye = (lax.broadcasted_iota(i32, (B, B), 0) == lax.broadcasted_iota(i32, (B, B), 1)).astype(f32).astype(bf16)
    for e in range(EXTENT):
        amat_t[e * B : (e + 1) * B, :] = nt(eye, amat[:, e * B : (e + 1) * B]).astype(bf16)

    lk, lz, lx, ly = log2(K4), log2(Z), log2(X), log2(Y)

    def row_of(k, zz, bb, aa, k_bits):
        yy = jnp.where(first, aa, bb)
        xx = jnp.where(first, bb, aa)
        per = 1 << k_bits
        return (
            (yy & 1) * (per * X * Y_HI * Z) + zz * (per * X * Y_HI) + (yy >> 1) * (per * X) + xx * per + k
        )

    LW = min(128, H)

    def perms(i):
        pos = i + lax.broadcasted_iota(i32, (CH, LW), 0)
        lane = lax.broadcasted_iota(i32, (CH, LW), 1)
        k = pos & (K4 - 1)
        half = (pos >> lk) & 1
        zp = (pos >> (lk + 1)) & (Z // 2 - 1)
        bb = (pos >> (lk + lz)) & 3
        aa = (pos >> (lk + lz + 2)) & 3
        rows = pl.ds(i, CH)
        for ref, zz in ((p4a, 2 * zp + half), (p4b, 2 * zp + 1 - half)):
            orig = row_of(k, zz, bb, aa, lk)
            for c in range(H // LW):
                ref[rows, c * LW : (c + 1) * LW] = jnp.where(orig == lane + c * LW, 1.0, 0.0).astype(bf16)

    loop(H, CH, perms)

    def perms8(i):
        pos = i + lax.broadcasted_iota(i32, (CH, LW), 0)
        lane = lax.broadcasted_iota(i32, (CH, LW), 1)
        k = pos & (2 * K4 - 1)
        zz = (pos >> (lk + 1)) & (Z - 1)
        bb = (pos >> (lk + 1 + lz)) & 3
        aa = (pos >> (lk + 3 + lz)) & 3
        orig = row_of(k, zz, bb, aa, lk + 1)
        for c in range(2 * H // LW):
            p8[pl.ds(i, CH), c * LW : (c + 1) * LW] = jnp.where(orig == lane + c * LW, 1.0, 0.0).astype(bf16)

    loop(2 * H, CH, perms8)
    s4_t[...] = nt(p4a[...], st[...]).astype(bf16)
    he_t[...] = nt(p4b[...], hid[...]).astype(bf16)
    tmp2[...] = nt(p8[:, :H], st[...])
    loads[4].wait()
    part[...] = mm(st[...], nw1[:H, :])
    own[...] = mm(amat[:, :R], msg[...].reshape(R, H))
    loads[5].wait()
    loads[6].wait()

    for j in range(4):

        @pl.when(has[j])
        def _():
            halo[back[j]].wait_recv()

    gath[...] = (own[...] + mm(amat[:, R:], ext[...].reshape(4 * B, H))).astype(bf16)
    part[...] += mm(gath[...], nw1[H:, :])

    def node_act(i):
        rows = pl.ds(i, CH)
        pre = part[rows, :] + nb1[...]
        g = jax.nn.sigmoid(pre)
        hid[rows, :] = (pre * g).astype(bf16)
        part[rows, :] = g * (1.0 + pre * (1.0 - g))

    loop(R, CH, node_act)
    tmp[...] = mm(hid[...], nw2[...])

    def norm(i):
        rows = pl.ds(i, CH)
        o = tmp[rows, :]
        centred = o - jnp.mean(o, axis=1, keepdims=True)
        inv = lax.rsqrt(jnp.mean(centred * centred, axis=1, keepdims=True) + norm_epsilon)
        normed = centred * inv
        fsv[rows, :] = (st[rows, :].astype(f32) + normed * gain[...]).astype(bf16)
        q = ct[rows, :].astype(f32) * gain[...]
        cot = inv * (
            q - jnp.mean(q, axis=1, keepdims=True) - normed * jnp.mean(q * normed, axis=1, keepdims=True)
        )
        cot_out[rows, :] = cot.astype(bf16)

    loop(R, CH, norm)
    out_fs = pltpu.make_async_copy(fsv, fs_h, out_sem.at[0])
    out_fs.start()
    tmp[...] = nt(cot_out[...], nw2[...])

    def node_slope(i):
        rows = pl.ds(i, CH)
        cot_pre[rows, :] = (tmp[rows, :] * part[rows, :]).astype(bf16)

    loop(R, CH, node_slope)
    cot_g[...] = nt(cot_pre[...], nw1[H:, :]).astype(bf16)

    rets[...] = mm(amat_t[R:, :], cot_g[...]).astype(bf16).reshape(4, B, H)
    home = [
        remote(rets.at[g], ret.at[back[g]], ret_ss.at[g], ret_rs.at[back[g]], sides[g]) for g in range(4)
    ]
    for g in range(4):

        @pl.when(has[g])
        def _():
            home[g].start()

    def halves(base, size, i, left, right):
        block = size // 4
        n_keep[pl.ds(pl.multiple_of(base + i, size), size), :] = jnp.where(first, left, right)
        sent = jnp.where(first, right, left).astype(bf16)
        for bb in range(4):
            rows = pl.ds(pl.multiple_of(base + bb * size + i // 4, block), block)
            n_r0s[rows, :] = sent[bb * block : (bb + 1) * block]

    hn_t[...] = nt(p4a[...], hid[...]).astype(bf16)
    sg8_t[...] = (tmp2[...] + nt(p8[:, H:], gath[...])).astype(bf16)
    own[...] = mm(amat_t[:R, :], cot_g[...])

    def grad_rows(base, size, left_ref, right_ref):
        def go(i):
            g = mm(left_ref[pl.ds(i, size), :], right_ref[...])
            halves(base, size, i, g[:, :HC], g[:, HC:])

        return go

    n1_rows, n2_rows = 2 * H // Y, H // Y
    loop(2 * H, n1_rows, grad_rows(0, n1_rows, sg8_t, cot_pre))
    loop(H, n2_rows, grad_rows(2 * H, n2_rows, hn_t, cot_out))
    n_rep = remote(n_r0s, n_r0, n_ss.at[0], n_rs.at[0], partner)
    n_rep.start()
    csp[...] = nt(cot_pre[...], nw1[:H, :])

    for j in range(4):

        @pl.when(has[j])
        def _():
            home[back[j]].wait_recv()

    def fold(i):
        rows = pl.ds(i, CH)
        for blk in range(BLK):
            full = pl.ds(pl.multiple_of(blk * B + i, CH), CH)
            total = own[full, :]
            for j in range(4):
                total = total + jnp.where(snd_s[j] == blk, ret[j, rows, :].astype(f32), 0.0)
            cot_msg[full, :] = total.astype(bf16)

    loop(B, CH, fold)

    tmp[...] = nt(cot_msg[...], ew2[...])

    def edge_slope(i):
        rows = pl.ds(i, CH)
        cot_pre_e[rows, :] = (tmp[rows, :] * slope[rows, :]).astype(bf16)

    loop(R, CH, edge_slope)

    def spread_stage(send, recv, ssem, rsem, base, me, count, peer):
        copies = []
        for j in range(1, count):
            copies.append(
                remote(
                    send.at[(me + j) % count], recv.at[j - 1], ssem.at[base + j - 1], rsem.at[base + j - 1], peer(j)
                )
            )
        return copies

    def gathered_sum(send, recv, me, count, rows):
        total = send[me, rows, :].astype(f32)
        for j in range(count - 1):
            total = total + recv[j, rows, :].astype(f32)
        return total

    n_rep.wait_recv()

    def n_first(i):
        for aa in range(Y):
            for base, size, off in ((0, n1_rows, 0), (2 * H, n2_rows, n1_rows)):
                step = size // 4
                rows = pl.ds(pl.multiple_of(base + aa * size + i * step, step), step)
                n_s1s[aa, pl.ds(pl.multiple_of(off + i * step, step), step), :] = (
                    n_keep[rows, :] + n_r0[rows, :].astype(f32)
                ).astype(bf16)

    lax.fori_loop(0, 4, lambda i, c: (n_first(i), c)[1], 0)
    n1 = spread_stage(n_s1s, n_s1, n_ss, n_rs, 1, a, Y, a_peer)
    for copy in n1:
        copy.start()

    sub = H // Y

    def e_grad(i):
        rows = pl.ds(i, sub)
        ga = mm(s4_t[rows, :], cot_pre_e[...])
        gb = mm(he_t[rows, :], cot_msg[...])
        lo = (lax.broadcasted_iota(i32, (sub, HC), 0) & (2 * K4 - 1)) < K4
        out = pl.multiple_of(2 * i, 2 * sub)
        for half in range(2):
            u, v = (ga, gb) if half == 0 else (gb, ga)
            left = jnp.where(lo, u[:, :HC], v[:, :HC])
            right = jnp.where(lo, u[:, HC:], v[:, HC:])
            at_rows = pl.ds(pl.multiple_of(out + half * sub, sub), sub)
            e_keep[at_rows, :] = jnp.where(first, left, right)
            sent = jnp.where(first, right, left).astype(bf16)
            block = sub // 4
            for bb in range(4):
                there = pl.ds(pl.multiple_of((2 * bb + half) * sub + i // 4, block), block)
                e_r0s[there, :] = sent[bb * block : (bb + 1) * block]

    loop(H, sub, e_grad)
    e_rep = remote(e_r0s, e_r0, e_ss.at[0], e_rs.at[0], partner)
    e_rep.start()

    csp[...] += nt(cot_pre_e[...], ew1[...])

    def finish_state(i):
        rows = pl.ds(i, CH)
        fsv2 = ct[rows, :].astype(f32) + csp[rows, :]
        ct[rows, :] = fsv2.astype(bf16)

    loop(R, CH, finish_state)
    out_sg = pltpu.make_async_copy(ct, sg_h, out_sem.at[1])
    out_sg.start()

    e_rep.wait_recv()

    def e_first(i):
        rows = pl.ds(i, sub)
        for aa in range(Y):
            full = pl.ds(pl.multiple_of(aa * 2 * sub + i, sub), sub)
            e_s1s[aa, rows, :] = (e_keep[full, :] + e_r0[full, :].astype(f32)).astype(bf16)

    loop(2 * sub, sub, e_first)
    e1 = spread_stage(e_s1s, e_s1, e_ss, e_rs, 1, a, Y, a_peer)
    for copy in e1:
        copy.start()

    for copy in n1:
        copy.wait_recv()
    zs = 2 * K4 * Z
    zh = K4 * Z
    for bb in range(X):
        n_s2s[bb, :zs, :] = gathered_sum(n_s1s, n_s1, a, Y, pl.ds(bb * zs, zs)).astype(bf16)
        n_s2s[bb, zs:, :] = gathered_sum(n_s1s, n_s1, a, Y, pl.ds(n1_rows + bb * zh, zh)).astype(bf16)
    n2 = spread_stage(n_s2s, n_s2, n_ss, n_rs, 4, b, X, b_peer)
    for copy in n2:
        copy.start()
    for copy in e1:
        copy.wait_recv()
    for bb in range(X):
        for half in range(2):
            e_s2s[bb, half * zh : (half + 1) * zh, :] = gathered_sum(
                e_s1s, e_s1, a, Y, pl.ds(half * sub + bb * zh, zh)
            ).astype(bf16)
    e2 = spread_stage(e_s2s, e_s2, e_ss, e_rs, 4, b, X, b_peer)
    for copy in e2:
        copy.start()

    k8 = 2 * K4
    for copy in n2:
        copy.wait_recv()
    nt_rows = gathered_sum(n_s2s, n_s2, b, X, pl.ds(0, zs + zh))
    for zz in range(Z):
        n_s3s[zz] = jnp.concatenate(
            [nt_rows[zz * k8 : (zz + 1) * k8], nt_rows[zs + (zz // 2) * k8 : zs + (zz // 2 + 1) * k8]], axis=0
        ).astype(bf16)
    n3 = spread_stage(n_s3s, n_s3, n_ss, n_rs, 7, z, Z, z_peer)
    for copy in n3:
        copy.start()
    for copy in e2:
        copy.wait_recv()
    et_rows = gathered_sum(e_s2s, e_s2, b, X, pl.ds(0, 2 * zh))
    for zz in range(Z):
        at_row = (zz % 2) * zh + (zz // 2) * k8
        e_s3s[zz] = et_rows[at_row : at_row + k8].astype(bf16)
    e3 = spread_stage(e_s3s, e_s3, e_ss, e_rs, 7, z, Z, z_peer)
    for copy in e3:
        copy.start()

    for copy in n3:
        copy.wait_recv()
    n_fs[...] = gathered_sum(n_s3s, n_s3, z, Z, pl.ds(0, 2 * k8))
    last = 6 + Z
    n_fin = remote(n_fs, n_f, n_ss.at[last], n_rs.at[last], partner)
    n_fin.start()
    for copy in e3:
        copy.wait_recv()
    e_fs[...] = gathered_sum(e_s3s, e_s3, z, Z, pl.ds(0, k8))
    e_fin = remote(e_fs, e_f, e_ss.at[last], e_rs.at[last], partner)
    e_fin.start()

    odd = (z % 2) == 1

    def whole(mine, theirs):
        u, v = mine[...], theirs[...]
        return jnp.concatenate([jnp.where(first, u, v), jnp.where(first, v, u)], axis=1)

    n_fin.wait_recv()
    full = whole(n_fs, n_f)
    gn1[...] = full[:k8]
    gn2[...] = jnp.where(odd, full[k8 + K4 :], full[k8 : k8 + K4])
    e_fin.wait_recv()
    full = whole(e_fs, e_f)
    ge1[...] = jnp.where(odd, full[K4:], full[:K4])
    ge2[...] = jnp.where(odd, full[:K4], full[K4:])

    out_fs.wait()
    out_sg.wait()
    for j in range(4):

        @pl.when(has[j])
        def _():
            halo[j].wait_send()
            home[j].wait_send()

    for copy in [n_rep, e_rep, n_fin, e_fin] + n1 + n2 + n3 + e1 + e2 + e3:
        copy.wait_send()


def make_body(Z, X):
    def body(
        node_state, node_cot, edge_w1, edge_b1, edge_w2, node_w1, node_b1, node_w2, norm_gain,
        tile_dst, tile_src, tile_count, tile_vals, send_blocks,
    ):
        R, H = node_state.shape[3:]
        T, B = tile_vals.shape[2:4]
        Y = Y_LO * Y_HI
        HC = H // 2
        K4 = H // (Z * X * Y)
        k8 = 2 * K4

        def v(shape, dtype=bf16):
            return pltpu.VMEM(shape, dtype)

        def stages(total, s1, s2, s3):
            return [
                v((total, HC), f32), v((total, HC)), v((total, HC)),
                v((Y, s1, HC)), v((Y - 1, s1, HC)),
                v((X, s2, HC)), v((X - 1, s2, HC)),
                v((Z, s3, HC)), v((Z - 1, s3, HC)),
                v((s3, HC), f32), v((s3, HC), f32),
            ]

        dma = pltpu.SemaphoreType.DMA
        scratch = [
            v((R, H)), v((R, H)), v((H, H)), v((H, H)), v((2 * H, H)), v((H, H)), v((T, B, B)), dma((7,)),
            v((R, H), f32), v((R, H)), v((BLK, B, H)), v((4, B, H)), v((4, B, H)), v((T, BLK * EXTENT, 8, B), f32),
            v((R, EXTENT * B)), v((EXTENT * B, R)), v((H, H)), v((H, H)), v((2 * H, 2 * H)),
            v((H, R)), v((H, R)), v((2 * H, R)), v((H, R)), v((R, H), f32), v((R, H)), v((R, H)), v((R, H)),
            v((R, H)), v((R, H), f32), v((R, H), f32), v((R, H), f32), v((2 * H, R), f32), v((R, H)),
            v((4, B, H)), v((4, B, H)), v((R, H)), v((R, H)),
        ]
        scratch += stages(3 * H, 3 * H // Y, 3 * H // (Y * X), 2 * k8)
        scratch += stages(2 * H, 2 * H // Y, 2 * H // (Y * X), k8)
        count = 7 + Z
        scratch += [dma((4,)), dma((4,)), dma((4,)), dma((4,))] + [dma((count,))] * 4 + [dma((2,))]
        smem = pl.BlockSpec(memory_space=pltpu.SMEM)
        vmem = pl.BlockSpec(memory_space=pltpu.VMEM)
        hbm = pl.BlockSpec(memory_space=pl.ANY)
        outs = pl.pallas_call(
            functools.partial(kernel, Z, X, H, B, T),
            out_shape=(
                jax.ShapeDtypeStruct((R, H), bf16),
                jax.ShapeDtypeStruct((R, H), bf16),
                jax.ShapeDtypeStruct((K4, H), f32),
                jax.ShapeDtypeStruct((K4, H), f32),
                jax.ShapeDtypeStruct((k8, H), f32),
                jax.ShapeDtypeStruct((K4, H), f32),
            ),
            in_specs=[smem] * 4 + [vmem] * 3 + [hbm] * 7,
            out_specs=[hbm] * 2 + [vmem] * 4,
            scratch_shapes=scratch,
            compiler_params=pltpu.CompilerParams(
                collective_id=0, has_side_effects=True, vmem_limit_bytes=60 * 1024 * 1024
            ),
            name="step",
        )(
            tile_dst.reshape(T), tile_src.reshape(T), tile_count.reshape(1), send_blocks.reshape(4),
            edge_b1.reshape(1, H), node_b1.reshape(1, H), norm_gain.reshape(1, H),
            node_state.reshape(R, H), node_cot.reshape(R, H), edge_w1.reshape(H, H), edge_w2.reshape(H, H),
            node_w1.reshape(2 * H, H), node_w2.reshape(H, H), tile_vals.reshape(T, B, B),
        )
        return (outs[0].reshape(node_state.shape), outs[1].reshape(node_state.shape)) + tuple(outs[2:])

    return body


def solution(mesh):
    in_specs = (
        P("rep", "stream", "span", None, None),
        P("rep", "stream", "span", None, None),
        P(), P(), P(), P(), P(), P(), P(),
        P("stream", "span", None),
        P("stream", "span", None),
        P("stream", "span"),
        P("stream", "span", None, None, None),
        P("stream", "span", None, None),
    )
    out_specs = (
        P("rep", "stream", "span", None, None),
        P("rep", "stream", "span", None, None),
        P(("stream", "span"), None),
        P(("stream", "span"), None),
        P(("stream", "span"), None),
        P(("stream", "span"), None),
    )
    body = make_body(mesh.shape["stream"] // Y_LO, mesh.shape["span"] // Y_HI)
    return jax.shard_map(body, mesh=mesh, in_specs=in_specs, out_specs=out_specs, check_vma=False)
```

```python
import functools

import jax
import jax.numpy as jnp
from jax import lax
from jax.experimental import pallas as pl
from jax.experimental.pallas import tpu as pltpu
from jax.sharding import PartitionSpec as P

norm_epsilon = 1e-05
f32, bf16, i32 = jnp.float32, jnp.bfloat16, jnp.int32
MESH = pl.DeviceIdType.MESH
Y_LO = 2
Y_HI = 2
BLK = 3
EXTENT = 7


def log2(n):
    assert n & (n - 1) == 0
    return n.bit_length() - 1


def mm(left_op, right_op):
    return jnp.dot(left_op, right_op, preferred_element_type=f32)


def nt(left_op, right_op):
    return lax.dot_general(left_op, right_op, (((1,), (1,)), ((), ())), preferred_element_type=f32)


def unrolled(total, step, fn):
    for i in range(0, total, step):
        fn(i)


def loop(total, step, fn):
    def trip(i, carry):
        fn(pl.multiple_of(i * step, step))
        return carry

    lax.fori_loop(0, total // step, trip, 0)


def kernel(
    Z, X, H, B, T,
    dst_h, src_h, cnt_h, snd_h, eb1_h, nb1_h, gain_h,
    st_h, ct_h, ew1_h, ew2_h, nw1_h, nw2_h, vals_h,
    states_h, grads,
    dst_s, src_s, cnt_s, snd_s, eb1, nb1, gain,
    st, ct, ew1, ew2, nw1, nw2, vals, in_sem,
    slope, hid, msg, ext, sendb, mask, amat, amat_t, p4, p8,
    he_t, s4_t, s8_t, g8_t, hn_t, part, gath, cot_out, cot_pre, cot_g, csp, own, tmp, fsv,
    rets, ret, cot_msg, cot_pre_e,
    n_keep, n_r0s, n_r0, n_s1s, n_s1, n_ts, n_t, n_s2s, n_s2, n_s3s, n_s3, n_fs, n_f,
    u_keep, u_r0s, u_r0, u_s1s, u_s1, u_ts, u_t, u_s2s, u_s2,
    v_keep, v_r0s, v_r0, v_s1s, v_s1, v_ts, v_t, v_s2s, v_s2,
    e_s3s, e_s3,
    halo_ss, halo_rs, ret_ss, ret_rs, n_ss, n_rs, u_ss, u_rs, v_ss, v_rs, e_ss, e_rs, out_sem,
):
    R = BLK * B
    HC = H // 2
    Y = Y_LO * Y_HI
    SHARDS = Z * X * Y
    K4 = H // SHARDS
    s = lax.axis_index("stream")
    p = lax.axis_index("span")
    r = lax.axis_index("rep")
    y_lo, z = s // Z, s % Z
    y_hi, x = p // X, p % X
    y = y_hi * Y_LO + y_lo
    first = r == 0
    a = jnp.where(first, y, x)
    b = jnp.where(first, x, y)
    has = (s > 0, s < Y_LO * Z - 1, p > 0, p < Y_HI * X - 1)

    def at(yy, xx, zz):
        return {"stream": (yy % Y_LO) * Z + zz, "span": (yy // Y_LO) * X + xx, "rep": r}

    a1, a3 = a + 1 - 2 * (a % 2), 3 - a
    a2 = (a + 2) % 4

    def a_at(aa):
        return at(jnp.where(first, aa, y), jnp.where(first, x, aa), z)

    def b_peer(j):
        return at(jnp.where(first, y, (y + j) % Y), jnp.where(first, (x + j) % X, x), z)

    def z_peer(j):
        return at(y, x, (z + j) % Z)

    def across(j):
        return {**z_peer(j), "rep": 1 - r}

    partner = {"stream": s, "span": p, "rep": 1 - r}
    sides = (
        {"stream": s - 1, "span": p, "rep": r},
        {"stream": s + 1, "span": p, "rep": r},
        {"stream": s, "span": p - 1, "rep": r},
        {"stream": s, "span": p + 1, "rep": r},
    )

    def remote(src, dst, ssem, rsem, dev):
        return pltpu.make_async_remote_copy(
            src_ref=src, dst_ref=dst, send_sem=ssem, recv_sem=rsem, device_id=dev, device_id_type=MESH
        )

    pairs = (
        (st_h, st), (ew1_h, ew1), (eb1_h, eb1), (snd_h, snd_s), (ew2_h, ew2),
        (dst_h, dst_s), (src_h, src_s), (cnt_h, cnt_s), (vals_h, vals),
        (nw1_h, nw1), (nb1_h, nb1), (nw2_h, nw2), (ct_h, ct), (gain_h, gain),
    )
    loads = [pltpu.make_async_copy(src, dst, in_sem.at[i]) for i, (src, dst) in enumerate(pairs)]
    for copy in loads[:5]:
        copy.start()

    def load(*which):
        for i in which:
            loads[i].wait()

    barrier = pltpu.get_barrier_semaphore()
    peers = [a_at(a1), a_at(a3)] + [b_peer(j) for j in range(1, 4)]
    peers += [z_peer(j) for j in range(1, Z)] + [across(j) for j in range(Z)]
    for dev in peers:
        pl.semaphore_signal(barrier, inc=1, device_id=dev, device_id_type=MESH)
    halo_count = 0
    for side in range(4):
        halo_count = halo_count + has[side].astype(i32)

        @pl.when(has[side])
        def _():
            pl.semaphore_signal(barrier, inc=1, device_id=sides[side], device_id_type=MESH)

    CH = min(32, B)
    load(0, 1, 2)
    for copy in loads[5:]:
        copy.start()
    tmp[...] = mm(st[...], ew1[...])

    def edge_act(i):
        rows = pl.ds(i, CH)
        pre = tmp[rows, :] + eb1[...]
        g = jax.nn.sigmoid(pre)
        hid[rows, :] = (pre * g).astype(bf16)
        slope[rows, :] = g * (1.0 + pre * (1.0 - g))

    unrolled(R, CH, edge_act)
    load(3, 4)
    tmp[...] = mm(hid[...], ew2[...])
    for blk in range(BLK):
        msg[blk] = tmp[blk * B : (blk + 1) * B, :].astype(bf16)
    for j in range(4):
        sendb[j] = msg[snd_s[0, j]]
    pl.semaphore_wait(barrier, len(peers) + halo_count)

    back = (1, 0, 3, 2)
    halo = [
        remote(sendb.at[j], ext.at[back[j]], halo_ss.at[j], halo_rs.at[back[j]], sides[j]) for j in range(4)
    ]
    for j in range(4):

        @pl.when(has[j])
        def _():
            halo[j].start()

        @pl.when(jnp.logical_not(has[j]))
        def _():
            ext[j] = jnp.zeros((B, H), bf16)
            ret[j] = jnp.zeros((B, H), bf16)

    def masks(t, carry):
        key = jnp.where(t < cnt_s[0, 0], dst_s[0, t] * EXTENT + src_s[0, t], -1)
        keys = jnp.full((16, B), key, i32)
        for q in range(BLK * EXTENT):
            mask[t, q] = jnp.where(keys == q, 1.0, 0.0).astype(bf16)
        return carry

    load(5, 6, 7)
    lax.fori_loop(0, T, masks, 0)
    load(8)

    def tiles(i):
        rows = pl.ds(i, CH)
        totals = [jnp.zeros((CH, B), bf16)] * (BLK * EXTENT)
        for t in range(T):
            v = vals[t, rows, :]
            totals = [
                total + jnp.concatenate([mask[t, q]] * (CH // 16), axis=0) * v for q, total in enumerate(totals)
            ]
        for q, total in enumerate(totals):
            d, e = q // EXTENT, q % EXTENT
            amat[pl.ds(pl.multiple_of(d * B + i, CH), CH), e * B : (e + 1) * B] = total

    loop(B, CH, tiles)
    eye = (lax.broadcasted_iota(i32, (B, B), 0) == lax.broadcasted_iota(i32, (B, B), 1)).astype(f32).astype(bf16)
    for e in range(EXTENT):
        amat_t[e * B : (e + 1) * B, :] = nt(eye, amat[:, e * B : (e + 1) * B]).astype(bf16)

    lk, lz = log2(K4), log2(Z)
    LW = min(128, H)

    def perms(i):
        pos = i + lax.broadcasted_iota(i32, (CH, LW), 0)
        lane = lax.broadcasted_iota(i32, (CH, LW), 1)
        zz = (pos >> lk) & (Z - 1)
        bb = (pos >> (lk + lz)) & 3
        aa = (pos >> (lk + lz + 2)) & 3
        yy, xx = jnp.where(first, aa, bb), jnp.where(first, bb, aa)
        four = (((yy & 1) * Z + zz) * Y_HI + (yy >> 1)) * (X * K4) + xx * K4 + (pos & (K4 - 1))
        zz = (pos >> (lk + 1)) & (Z - 1)
        q = (pos >> (lk + 1 + lz)) & (2 * X - 1)
        yh, xx = jnp.where(first, q >> 2, q & 1), jnp.where(first, q & 3, q >> 1)
        eight = (zz * Y_HI + yh) * (2 * X * K4) + xx * (2 * K4) + (pos & (2 * K4 - 1))
        rows = pl.ds(i, CH)
        for ref, orig in ((p4, four), (p8, eight)):
            for c in range(H // LW):
                ref[rows, c * LW : (c + 1) * LW] = jnp.where(orig == lane + c * LW, 1.0, 0.0).astype(bf16)

    loop(H, CH, perms)
    he_t[...] = nt(p4[...], hid[...]).astype(bf16)
    s8_t[...] = nt(p8[...], st[...]).astype(bf16)
    load(9, 10)
    part[...] = mm(st[...], nw1[:H, :])
    own[...] = mm(amat[:, :R], msg[...].reshape(R, H))
    load(11, 12, 13)

    for j in range(4):

        @pl.when(has[j])
        def _():
            halo[back[j]].wait_recv()

    gath[...] = (own[...] + mm(amat[:, R:], ext[...].reshape(4 * B, H))).astype(bf16)
    part[...] += mm(gath[...], nw1[H:, :])

    def node_act(i):
        rows = pl.ds(i, CH)
        pre = part[rows, :] + nb1[...]
        g = jax.nn.sigmoid(pre)
        hid[rows, :] = (pre * g).astype(bf16)
        part[rows, :] = g * (1.0 + pre * (1.0 - g))

    unrolled(R, CH, node_act)
    tmp[...] = mm(hid[...], nw2[...])

    def norm(i):
        rows = pl.ds(i, CH)
        o = tmp[rows, :]
        centred = o - jnp.mean(o, axis=1, keepdims=True)
        inv = lax.rsqrt(jnp.mean(centred * centred, axis=1, keepdims=True) + norm_epsilon)
        normed = centred * inv
        fsv[rows, :] = (st[rows, :].astype(f32) + normed * gain[...]).astype(bf16)
        q = ct[rows, :].astype(f32) * gain[...]
        cot = inv * (
            q - jnp.mean(q, axis=1, keepdims=True) - normed * jnp.mean(q * normed, axis=1, keepdims=True)
        )
        cot_out[rows, :] = cot.astype(bf16)

    unrolled(R, CH, norm)
    out_fs = pltpu.make_async_copy(fsv, states_h.at[0], out_sem.at[0])
    out_fs.start()
    tmp[...] = nt(cot_out[...], nw2[...])

    def node_slope(i):
        rows = pl.ds(i, CH)
        cot_pre[rows, :] = (tmp[rows, :] * part[rows, :]).astype(bf16)

    unrolled(R, CH, node_slope)
    cot_g[...] = nt(cot_pre[...], nw1[H:, :]).astype(bf16)

    rets[...] = mm(amat_t[R:, :], cot_g[...]).astype(bf16).reshape(4, B, H)
    home = [
        remote(rets.at[g], ret.at[back[g]], ret_ss.at[g], ret_rs.at[back[g]], sides[g]) for g in range(4)
    ]
    for g in range(4):

        @pl.when(has[g])
        def _():
            home[g].start()

    hn_t[...] = nt(p4[...], hid[...]).astype(bf16)
    g8_t[...] = nt(p8[...], gath[...]).astype(bf16)
    z8, z4 = 2 * K4 * Z, K4 * Z

    def n1_grad(i):
        for y_low, left in ((0, s8_t), (1, g8_t)):
            g = mm(left[pl.ds(i, 2 * z8), :], cot_pre[...])
            sent = jnp.where(first, g[:, HC:], g[:, :HC]).astype(bf16)
            kept = jnp.where(first, g[:, :HC], g[:, HC:])
            for half in range(2):
                q = i // z8 + half
                yy = jnp.where(first, q // 4, q % 2) * 2 + y_low
                xx = jnp.where(first, q % 4, q // 2)
                aa, bb = jnp.where(first, yy, xx), jnp.where(first, xx, yy)
                block = slice(half * z8, (half + 1) * z8)
                n_keep[pl.ds(pl.multiple_of((aa * 4 + bb) * z8, z8), z8), :] = kept[block]
                n_r0s[pl.ds(pl.multiple_of((bb * 4 + aa) * z8, z8), z8), :] = sent[block]

    unrolled(H, 2 * z8, n1_grad)

    def four_rows(base, left, right, keep, send):
        def go(i):
            g = mm(left[pl.ds(i, 4 * z4), :], right[...])
            keep[pl.ds(base + i, 4 * z4), :] = jnp.where(first, g[:, :HC], g[:, HC:])
            sent = jnp.where(first, g[:, HC:], g[:, :HC]).astype(bf16)
            for bb in range(4):
                rows = pl.ds(base + bb * 4 * z4 + i // 4, z4)
                send[rows, :] = sent[bb * z4 : (bb + 1) * z4]

        unrolled(H, 4 * z4, go)

    four_rows(2 * H, hn_t, cot_out, n_keep, n_r0s)
    n_rep = remote(n_r0s, n_r0, n_ss.at[0], n_rs.at[0], partner)
    n_rep.start()
    own[...] = mm(amat_t[:R, :], cot_g[...])
    csp[...] = nt(cot_pre[...], nw1[:H, :])
    s4_t[...] = nt(p4[...], st[...]).astype(bf16)

    QC = HC // 2

    def add_partner(parts, keep, got, send):
        def go(i):
            for aa in range(4):
                off = 0
                for base, size in parts:
                    step = size // 4
                    rows = pl.ds(pl.multiple_of(base + aa * size + i * step, step), step)
                    total = (keep[rows, :] + got[rows, :].astype(f32)).astype(bf16)
                    there = pl.ds(pl.multiple_of(off + i * step, step), step)
                    send[0, aa, there, :] = total[:, :QC]
                    send[1, aa, there, :] = total[:, QC:]
                    off += size

        lax.fori_loop(0, 4, lambda i, c: (go(i), c)[1], 0)

    def first_step(send, recv, ss, rs):
        copies = []
        for half, near in ((0, a1), (1, a3)):
            for slot, chunk in ((1, a2), (0, near)):
                k = 1 + 2 * half + slot
                copies.append(
                    remote(send.at[half, chunk], recv.at[half, slot], ss.at[k], rs.at[k], a_at(near))
                )
        for copy in copies:
            copy.start()
        return copies

    def second_step(copies, send, recv, mid_s, mid_r, ss, rs):
        for copy in copies:
            copy.wait_recv()
        more = []
        for half, near in ((0, a3), (1, a1)):
            mid_s[half] = (send[half, near].astype(f32) + recv[half, 1].astype(f32)).astype(bf16)
            k = 5 + half
            copy = remote(mid_s.at[half], mid_r.at[half], ss.at[k], rs.at[k], a_at(near))
            copy.start()
            more.append(copy)
        return more

    def b_stage(copies, send, recv, mid_r, out, got, parts, ss, rs):
        for copy in copies:
            copy.wait_recv()
        for bb in range(4):
            lo = 0
            off = 0
            for size in parts:
                rows = pl.ds(lo + bb * (size // 4), size // 4)
                halves = [
                    send[h, a, rows, :].astype(f32) + recv[h, 0, rows, :].astype(f32) + mid_r[h, rows, :].astype(f32)
                    for h in range(2)
                ]
                out[bb, off : off + size // 4, :] = jnp.concatenate(halves, axis=1).astype(bf16)
                lo += size
                off += size // 4
        more = [
            remote(out.at[(b + j) % 4], got.at[j - 1], ss.at[6 + j], rs.at[6 + j], b_peer(j)) for j in (2, 1, 3)
        ]
        for copy in more:
            copy.start()
        return more

    def b_sum(copies, send, recv):
        for copy in copies:
            copy.wait_recv()
        total = send[b].astype(f32)
        for j in range(3):
            total = total + recv[j].astype(f32)
        return total

    n_parts, e_parts = ((0, 2 * H // 4), (2 * H, H // 4)), ((0, H // 4),)
    n_sizes, e_sizes = (2 * H // 4, H // 4), (H // 4,)
    k8 = 2 * K4

    n_rep.wait_recv()
    add_partner(n_parts, n_keep, n_r0, n_s1s)
    n1 = first_step(n_s1s, n_s1, n_ss, n_rs)

    for j in range(4):

        @pl.when(has[j])
        def _():
            home[back[j]].wait_recv()

    def fold(i):
        rows = pl.ds(i, CH)
        for blk in range(BLK):
            full = pl.ds(blk * B + i, CH)
            total = own[full, :]
            for j in range(4):
                total = total + jnp.where(snd_s[0, j] == blk, ret[j, rows, :].astype(f32), 0.0)
            cot_msg[full, :] = total.astype(bf16)

    unrolled(B, CH, fold)

    four_rows(0, he_t, cot_msg, u_keep, u_r0s)
    u_rep = remote(u_r0s, u_r0, u_ss.at[0], u_rs.at[0], partner)
    u_rep.start()
    n2 = second_step(n1, n_s1s, n_s1, n_ts, n_t, n_ss, n_rs)
    tmp[...] = nt(cot_msg[...], ew2[...])

    def edge_slope(i):
        rows = pl.ds(i, CH)
        cot_pre_e[rows, :] = (tmp[rows, :] * slope[rows, :]).astype(bf16)

    unrolled(R, CH, edge_slope)
    four_rows(0, s4_t, cot_pre_e, v_keep, v_r0s)
    v_rep = remote(v_r0s, v_r0, v_ss.at[0], v_rs.at[0], partner)
    v_rep.start()
    u_rep.wait_recv()
    add_partner(e_parts, u_keep, u_r0, u_s1s)
    u1 = first_step(u_s1s, u_s1, u_ss, u_rs)

    csp[...] += nt(cot_pre_e[...], ew1[...])

    def finish_state(i):
        rows = pl.ds(i, CH)
        ct[rows, :] = (ct[rows, :].astype(f32) + csp[rows, :]).astype(bf16)

    unrolled(R, CH, finish_state)
    out_sg = pltpu.make_async_copy(ct, states_h.at[1], out_sem.at[1])
    out_sg.start()

    v_rep.wait_recv()
    add_partner(e_parts, v_keep, v_r0, v_s1s)
    v1 = first_step(v_s1s, v_s1, v_ss, v_rs)

    n3 = b_stage(n2, n_s1s, n_s1, n_t, n_s2s, n_s2, n_sizes, n_ss, n_rs)
    u2 = second_step(u1, u_s1s, u_s1, u_ts, u_t, u_ss, u_rs)
    v2 = second_step(v1, v_s1s, v_s1, v_ts, v_t, v_ss, v_rs)
    u3 = b_stage(u2, u_s1s, u_s1, u_t, u_s2s, u_s2, e_sizes, u_ss, u_rs)
    v3 = b_stage(v2, v_s1s, v_s1, v_t, v_s2s, v_s2, e_sizes, v_ss, v_rs)

    rows_n = b_sum(n3, n_s2s, n_s2)
    for zz in range(Z):
        pair = z8 + (zz // 2) * k8
        n_s3s[zz] = jnp.concatenate([rows_n[zz * k8 : (zz + 1) * k8], rows_n[pair : pair + k8]], axis=0).astype(bf16)
    n4 = []
    for j in range(1, Z):
        k = 9 + j
        n4.append(remote(n_s3s.at[(z + j) % Z], n_s3.at[j - 1], n_ss.at[k], n_rs.at[k], z_peer(j)))
    for copy in n4:
        copy.start()
    rows_u = b_sum(u3, u_s2s, u_s2)
    rows_v = b_sum(v3, v_s2s, v_s2)
    for zz in range(Z):
        e_s3s[zz] = jnp.concatenate(
            [rows_v[zz * K4 : (zz + 1) * K4], rows_u[zz * K4 : (zz + 1) * K4]], axis=0
        ).astype(bf16)
    e4 = []
    for j in range(1, Z):
        e4.append(remote(e_s3s.at[(z + j) % Z], e_s3.at[0, j], e_ss.at[j], e_rs.at[j], z_peer(j)))
    for j in range(Z):
        e4.append(remote(e_s3s.at[(z + j) % Z], e_s3.at[1, j], e_ss.at[Z + j], e_rs.at[Z + j], across(j)))
    for copy in e4:
        copy.start()

    def whole(mine, theirs):
        return jnp.concatenate([jnp.where(first, mine, theirs), jnp.where(first, theirs, mine)], axis=1)

    for copy in n4:
        copy.wait_recv()
    total = n_s3s[z].astype(f32)
    for j in range(Z - 1):
        total = total + n_s3[j].astype(f32)
    n_fs[...] = total
    n_fin = remote(n_fs, n_f, n_ss.at[9 + Z], n_rs.at[9 + Z], partner)
    n_fin.start()
    n_fin.wait_recv()
    full = whole(n_fs[...], n_f[...])
    grads[:k8, :] = full[:k8]
    grads[k8 : k8 + K4, :] = jnp.where(z % 2 == 1, full[k8 + K4 :], full[k8 : k8 + K4])
    for copy in e4:
        copy.wait_recv()
    mine, theirs = e_s3s[z].astype(f32), e_s3[1, 0].astype(f32)
    for j in range(1, Z):
        mine = mine + e_s3[0, j].astype(f32)
        theirs = theirs + e_s3[1, j].astype(f32)
    grads[2 * k8 :, :] = whole(mine, theirs)

    out_fs.wait()
    out_sg.wait()
    for j in range(4):

        @pl.when(has[j])
        def _():
            halo[j].wait_send()
            home[j].wait_send()

    for copy in [n_rep, u_rep, v_rep, n_fin] + n1 + n2 + n3 + n4 + u1 + u2 + u3 + v1 + v2 + v3 + e4:
        copy.wait_send()


def deliver(K4, states_h, grads, fs_h, sg_h, ge1, ge2, gn1, gn2, buf, sem):
    into = [pltpu.make_async_copy(states_h.at[i], buf.at[i], sem.at[i]) for i in range(2)]
    out = [pltpu.make_async_copy(buf.at[i], ref, sem.at[2 + i]) for i, ref in enumerate((fs_h, sg_h))]
    for copy in into:
        copy.start()
    gn1[...] = grads[: 2 * K4, :]
    gn2[...] = grads[2 * K4 : 3 * K4, :]
    ge1[...] = grads[4 * K4 : 5 * K4, :]
    ge2[...] = grads[5 * K4 :, :]
    for i in range(2):
        into[i].wait()
        out[i].start()
    for i in range(2):
        out[i].wait()


def make_body(Z, X):
    def body(
        node_state, node_cot, edge_w1, edge_b1, edge_w2, node_w1, node_b1, node_w2, norm_gain,
        tile_dst, tile_src, tile_count, tile_vals, send_blocks,
    ):
        R, H = node_state.shape[3:]
        T, B = tile_vals.shape[2:4]
        Y = Y_LO * Y_HI
        HC = H // 2
        K4 = H // (Z * X * Y)
        k8 = 2 * K4

        def v(shape, dtype=bf16):
            return pltpu.VMEM(shape, dtype)

        def stages(total, s1, s2):
            return [
                v((total, HC), f32), v((total, HC)), v((total, HC)),
                v((2, 4, s1, HC // 2)), v((2, 2, s1, HC // 2)), v((2, s1, HC // 2)), v((2, s1, HC // 2)),
                v((4, s2, HC)), v((3, s2, HC)),
            ]

        dma = pltpu.SemaphoreType.DMA
        scratch = [pltpu.SMEM((1, T), i32), pltpu.SMEM((1, T), i32), pltpu.SMEM((1, 1), i32), pltpu.SMEM((1, 4), i32)]
        scratch += [v((1, H), f32)] * 3
        scratch += [
            v((R, H)), v((R, H)), v((H, H)), v((H, H)), v((2 * H, H)), v((H, H)), v((T, B, B)), dma((14,)),
            v((R, H), f32), v((R, H)), v((BLK, B, H)), v((4, B, H)), v((4, B, H)), v((T, BLK * EXTENT, 16, B)),
            v((R, EXTENT * B)), v((EXTENT * B, R)), v((H, H)), v((H, H)),
            v((H, R)), v((H, R)), v((H, R)), v((H, R)), v((H, R)), v((R, H), f32), v((R, H)), v((R, H)), v((R, H)),
            v((R, H)), v((R, H), f32), v((R, H), f32), v((R, H), f32), v((R, H)),
            v((4, B, H)), v((4, B, H)), v((R, H)), v((R, H)),
        ]
        scratch += stages(3 * H, 3 * H // 4, 3 * H // 16)
        scratch += [v((Z, 2 * k8, HC)), v((Z - 1, 2 * k8, HC)), v((2 * k8, HC), f32), v((2 * k8, HC), f32)]
        scratch += stages(H, H // 4, H // 16) * 2
        scratch += [v((Z, k8, HC)), v((2, Z, k8, HC))]
        scratch += [dma((4,))] * 4 + [dma((10 + Z,))] * 2 + [dma((10,))] * 4 + [dma((2 * Z,))] * 2 + [dma((2,))]
        vmem = pl.BlockSpec(memory_space=pltpu.VMEM)
        hbm = pl.BlockSpec(memory_space=pl.ANY)
        states, grads = pl.pallas_call(
            functools.partial(kernel, Z, X, H, B, T),
            out_shape=(jax.ShapeDtypeStruct((2, R, H), bf16), jax.ShapeDtypeStruct((6 * K4, H), f32)),
            in_specs=[hbm] * 14,
            out_specs=(hbm, vmem),
            scratch_shapes=scratch,
            compiler_params=pltpu.CompilerParams(
                collective_id=0, has_side_effects=True, vmem_limit_bytes=60 * 1024 * 1024
            ),
            name="step",
        )(
            tile_dst.reshape(1, T), tile_src.reshape(1, T), tile_count, send_blocks.reshape(1, 4),
            edge_b1.reshape(1, H), node_b1.reshape(1, H), norm_gain.reshape(1, H),
            node_state.reshape(R, H), node_cot.reshape(R, H), edge_w1.reshape(H, H), edge_w2.reshape(H, H),
            node_w1.reshape(2 * H, H), node_w2.reshape(H, H), tile_vals.reshape(T, B, B),
        )
        outs = pl.pallas_call(
            functools.partial(deliver, K4),
            out_shape=(
                jax.ShapeDtypeStruct((R, H), bf16),
                jax.ShapeDtypeStruct((R, H), bf16),
                jax.ShapeDtypeStruct((K4, H), f32),
                jax.ShapeDtypeStruct((K4, H), f32),
                jax.ShapeDtypeStruct((k8, H), f32),
                jax.ShapeDtypeStruct((K4, H), f32),
            ),
            in_specs=[hbm, vmem],
            out_specs=[hbm] * 2 + [vmem] * 4,
            scratch_shapes=[v((2, R, H)), dma((4,))],
            name="deliver",
        )(states, grads)
        return (outs[0].reshape(node_state.shape), outs[1].reshape(node_state.shape)) + tuple(outs[2:])

    return body


def solution(mesh):
    in_specs = (
        P("rep", "stream", "span", None, None),
        P("rep", "stream", "span", None, None),
        P(), P(), P(), P(), P(), P(), P(),
        P("stream", "span", None),
        P("stream", "span", None),
        P("stream", "span"),
        P("stream", "span", None, None, None),
        P("stream", "span", None, None),
    )
    out_specs = (
        P("rep", "stream", "span", None, None),
        P("rep", "stream", "span", None, None),
        P(("stream", "span"), None),
        P(("stream", "span"), None),
        P(("stream", "span"), None),
        P(("stream", "span"), None),
    )
    body = make_body(mesh.shape["stream"] // Y_LO, mesh.shape["span"] // Y_HI)
    return jax.shard_map(body, mesh=mesh, in_specs=in_specs, out_specs=out_specs, check_vma=False)
```

```python
import functools

import jax
import jax.numpy as jnp
from jax import lax
from jax.experimental import pallas as pl
from jax.experimental.pallas import tpu as pltpu
from jax.sharding import PartitionSpec as P

norm_epsilon = 1e-05
f32, bf16, i32 = jnp.float32, jnp.bfloat16, jnp.int32
MESH = pl.DeviceIdType.MESH
Y_LO = 2
Y_HI = 2
BLK = 3
EXTENT = 7


def log2(n):
    assert n & (n - 1) == 0
    return n.bit_length() - 1


def mm(left_op, right_op):
    return jnp.dot(left_op, right_op, preferred_element_type=f32)


def nt(left_op, right_op):
    return lax.dot_general(left_op, right_op, (((1,), (1,)), ((), ())), preferred_element_type=f32)


def unrolled(total, step, fn):
    for i in range(0, total, step):
        fn(i)


def loop(total, step, fn):
    def trip(i, carry):
        fn(pl.multiple_of(i * step, step))
        return carry

    lax.fori_loop(0, total // step, trip, 0)


def kernel(
    Z, X, H, B, T,
    dst_h, src_h, cnt_h, snd_h, eb1_h, nb1_h, gain_h,
    st_h, ct_h, ew1_h, ew2_h, nw1_h, nw2_h, vals_h,
    states_h, grads,
    dst_s, src_s, cnt_s, snd_s, eb1, nb1, gain,
    st, ct, ew1, ew2, nw1, nw2, vals, in_sem,
    slope, hid, msg, ext, sendb, mask, amat, amat_t, p4, p8,
    he_t, s4_t, s8_t, g8_t, hn_t, part, gath, cot_out, cot_pre, cot_g, csp, own, tmp, fsv,
    rets, ret, cot_msg, cot_pre_e,
    n_keep, n_r0s, n_r0, n_s1s, n_s1, n_ts, n_t, n_s2s, n_s2, n_s3s, n_s3, n_fs, n_f,
    u_keep, u_r0s, u_r0, u_s1s, u_s1, u_ts, u_t, u_s2s, u_s2,
    v_keep, v_r0s, v_r0, v_s1s, v_s1, v_ts, v_t, v_s2s, v_s2,
    e_s3s, e_s3,
    halo_ss, halo_rs, ret_ss, ret_rs, n_ss, n_rs, u_ss, u_rs, v_ss, v_rs, e_ss, e_rs, out_sem,
):
    R = BLK * B
    HC = H // 2
    Y = Y_LO * Y_HI
    SHARDS = Z * X * Y
    K4 = H // SHARDS
    s = lax.axis_index("stream")
    p = lax.axis_index("span")
    r = lax.axis_index("rep")
    y_lo, z = s // Z, s % Z
    y_hi, x = p // X, p % X
    y = y_hi * Y_LO + y_lo
    first = r == 0
    a = jnp.where(first, y, x)
    b = jnp.where(first, x, y)
    has = (s > 0, s < Y_LO * Z - 1, p > 0, p < Y_HI * X - 1)

    def at(yy, xx, zz):
        return {"stream": (yy % Y_LO) * Z + zz, "span": (yy // Y_LO) * X + xx, "rep": r}

    a1, a3 = a + 1 - 2 * (a % 2), 3 - a
    a2 = (a + 2) % 4

    def a_at(aa):
        return at(jnp.where(first, aa, y), jnp.where(first, x, aa), z)

    def b_peer(j):
        return at(jnp.where(first, y, (y + j) % Y), jnp.where(first, (x + j) % X, x), z)

    def z_peer(j):
        return at(y, x, (z + j) % Z)

    def across(j):
        return {**z_peer(j), "rep": 1 - r}

    partner = {"stream": s, "span": p, "rep": 1 - r}
    sides = (
        {"stream": s - 1, "span": p, "rep": r},
        {"stream": s + 1, "span": p, "rep": r},
        {"stream": s, "span": p - 1, "rep": r},
        {"stream": s, "span": p + 1, "rep": r},
    )

    def remote(src, dst, ssem, rsem, dev):
        return pltpu.make_async_remote_copy(
            src_ref=src, dst_ref=dst, send_sem=ssem, recv_sem=rsem, device_id=dev, device_id_type=MESH
        )

    pairs = (
        (st_h, st), (ew1_h, ew1), (eb1_h, eb1), (snd_h, snd_s), (ew2_h, ew2),
        (dst_h, dst_s), (src_h, src_s), (cnt_h, cnt_s), (vals_h, vals),
        (nw1_h, nw1), (nb1_h, nb1), (nw2_h, nw2), (ct_h, ct), (gain_h, gain),
    )
    loads = [pltpu.make_async_copy(src, dst, in_sem.at[i]) for i, (src, dst) in enumerate(pairs)]
    for copy in loads[:5]:
        copy.start()

    def load(*which):
        for i in which:
            loads[i].wait()

    barrier = pltpu.get_barrier_semaphore()
    peers = [a_at(a1), a_at(a3)] + [b_peer(j) for j in range(1, 4)]
    peers += [z_peer(j) for j in range(1, Z)] + [across(j) for j in range(Z)]
    for dev in peers:
        pl.semaphore_signal(barrier, inc=1, device_id=dev, device_id_type=MESH)
    halo_count = 0
    for side in range(4):
        halo_count = halo_count + has[side].astype(i32)

        @pl.when(has[side])
        def _():
            pl.semaphore_signal(barrier, inc=1, device_id=sides[side], device_id_type=MESH)

    CH = min(32, B)
    load(0, 1, 2)
    for copy in loads[5:]:
        copy.start()
    tmp[...] = mm(st[...], ew1[...])

    def edge_act(i):
        rows = pl.ds(i, CH)
        pre = tmp[rows, :] + eb1[...]
        g = jax.nn.sigmoid(pre)
        hid[rows, :] = (pre * g).astype(bf16)
        slope[rows, :] = g * (1.0 + pre * (1.0 - g))

    unrolled(R, CH, edge_act)
    load(3, 4)
    tmp[...] = mm(hid[...], ew2[...])
    for blk in range(BLK):
        msg[blk] = tmp[blk * B : (blk + 1) * B, :].astype(bf16)
    for j in range(4):
        sendb[j] = msg[snd_s[0, j]]
    pl.semaphore_wait(barrier, len(peers) + halo_count)

    back = (1, 0, 3, 2)
    halo = [
        remote(sendb.at[j], ext.at[back[j]], halo_ss.at[j], halo_rs.at[back[j]], sides[j]) for j in range(4)
    ]
    for j in range(4):

        @pl.when(has[j])
        def _():
            halo[j].start()

        @pl.when(jnp.logical_not(has[j]))
        def _():
            ext[j] = jnp.zeros((B, H), bf16)
            ret[j] = jnp.zeros((B, H), bf16)

    def masks(t, carry):
        key = jnp.where(t < cnt_s[0, 0], dst_s[0, t] * EXTENT + src_s[0, t], -1)
        keys = jnp.full((16, B), key, i32)
        for q in range(BLK * EXTENT):
            mask[t, q] = jnp.where(keys == q, 1.0, 0.0).astype(bf16)
        return carry

    load(5, 6, 7)
    lax.fori_loop(0, T, masks, 0)
    load(8)

    def tiles(i):
        rows = pl.ds(i, CH)
        totals = [jnp.zeros((CH, B), bf16)] * (BLK * EXTENT)
        for t in range(T):
            v = vals[t, rows, :]
            totals = [
                total + jnp.concatenate([mask[t, q]] * (CH // 16), axis=0) * v for q, total in enumerate(totals)
            ]
        for q, total in enumerate(totals):
            d, e = q // EXTENT, q % EXTENT
            amat[pl.ds(pl.multiple_of(d * B + i, CH), CH), e * B : (e + 1) * B] = total

    loop(B, CH, tiles)
    eye = (lax.broadcasted_iota(i32, (B, B), 0) == lax.broadcasted_iota(i32, (B, B), 1)).astype(f32).astype(bf16)
    for e in range(EXTENT):
        amat_t[e * B : (e + 1) * B, :] = nt(eye, amat[:, e * B : (e + 1) * B]).astype(bf16)

    lk, lz = log2(K4), log2(Z)
    LW = min(128, H)

    def perms(i):
        pos = i + lax.broadcasted_iota(i32, (CH, LW), 0)
        lane = lax.broadcasted_iota(i32, (CH, LW), 1)
        zz = (pos >> lk) & (Z - 1)
        bb = (pos >> (lk + lz)) & 3
        aa = (pos >> (lk + lz + 2)) & 3
        yy, xx = jnp.where(first, aa, bb), jnp.where(first, bb, aa)
        four = (((yy & 1) * Z + zz) * Y_HI + (yy >> 1)) * (X * K4) + xx * K4 + (pos & (K4 - 1))
        zz = (pos >> (lk + 1)) & (Z - 1)
        q = (pos >> (lk + 1 + lz)) & (2 * X - 1)
        yh, xx = jnp.where(first, q >> 2, q & 1), jnp.where(first, q & 3, q >> 1)
        eight = (zz * Y_HI + yh) * (2 * X * K4) + xx * (2 * K4) + (pos & (2 * K4 - 1))
        rows = pl.ds(i, CH)
        for ref, orig in ((p4, four), (p8, eight)):
            for c in range(H // LW):
                ref[rows, c * LW : (c + 1) * LW] = jnp.where(orig == lane + c * LW, 1.0, 0.0).astype(bf16)

    loop(H, CH, perms)
    he_t[...] = nt(p4[...], hid[...]).astype(bf16)
    s8_t[...] = nt(p8[...], st[...]).astype(bf16)
    load(9, 10)
    part[...] = mm(st[...], nw1[:H, :])
    own[...] = mm(amat[:, :R], msg[...].reshape(R, H))
    load(11, 12, 13)

    for j in range(4):

        @pl.when(has[j])
        def _():
            halo[back[j]].wait_recv()

    gath[...] = (own[...] + mm(amat[:, R:], ext[...].reshape(4 * B, H))).astype(bf16)
    part[...] += mm(gath[...], nw1[H:, :])

    def node_act(i):
        rows = pl.ds(i, CH)
        pre = part[rows, :] + nb1[...]
        g = jax.nn.sigmoid(pre)
        hid[rows, :] = (pre * g).astype(bf16)
        part[rows, :] = g * (1.0 + pre * (1.0 - g))

    unrolled(R, CH, node_act)
    tmp[...] = mm(hid[...], nw2[...])

    def norm(i):
        rows = pl.ds(i, CH)
        o = tmp[rows, :]
        centred = o - jnp.mean(o, axis=1, keepdims=True)
        inv = lax.rsqrt(jnp.mean(centred * centred, axis=1, keepdims=True) + norm_epsilon)
        normed = centred * inv
        fsv[rows, :] = (st[rows, :].astype(f32) + normed * gain[...]).astype(bf16)
        q = ct[rows, :].astype(f32) * gain[...]
        cot = inv * (
            q - jnp.mean(q, axis=1, keepdims=True) - normed * jnp.mean(q * normed, axis=1, keepdims=True)
        )
        cot_out[rows, :] = cot.astype(bf16)

    unrolled(R, CH, norm)
    out_fs = pltpu.make_async_copy(fsv, states_h.at[0], out_sem.at[0])
    out_fs.start()
    tmp[...] = nt(cot_out[...], nw2[...])

    def node_slope(i):
        rows = pl.ds(i, CH)
        cot_pre[rows, :] = (tmp[rows, :] * part[rows, :]).astype(bf16)

    unrolled(R, CH, node_slope)
    cot_g[...] = nt(cot_pre[...], nw1[H:, :]).astype(bf16)

    rets[...] = mm(amat_t[R:, :], cot_g[...]).astype(bf16).reshape(4, B, H)
    home = [
        remote(rets.at[g], ret.at[back[g]], ret_ss.at[g], ret_rs.at[back[g]], sides[g]) for g in range(4)
    ]
    for g in range(4):

        @pl.when(has[g])
        def _():
            home[g].start()

    hn_t[...] = nt(p4[...], hid[...]).astype(bf16)
    g8_t[...] = nt(p8[...], gath[...]).astype(bf16)
    z8, z4 = 2 * K4 * Z, K4 * Z

    def n1_grad(i):
        for y_low, left in ((0, s8_t), (1, g8_t)):
            g = mm(left[pl.ds(i, 2 * z8), :], cot_pre[...])
            sent = jnp.where(first, g[:, HC:], g[:, :HC]).astype(bf16)
            kept = jnp.where(first, g[:, :HC], g[:, HC:])
            for half in range(2):
                q = i // z8 + half
                yy = jnp.where(first, q // 4, q % 2) * 2 + y_low
                xx = jnp.where(first, q % 4, q // 2)
                aa, bb = jnp.where(first, yy, xx), jnp.where(first, xx, yy)
                block = slice(half * z8, (half + 1) * z8)
                n_keep[pl.ds(pl.multiple_of((aa * 4 + bb) * z8, z8), z8), :] = kept[block]
                n_r0s[pl.ds(pl.multiple_of((bb * 4 + aa) * z8, z8), z8), :] = sent[block]

    unrolled(H, 2 * z8, n1_grad)

    def four_rows(base, left, right, keep, send):
        def go(i):
            g = mm(left[pl.ds(i, 4 * z4), :], right[...])
            keep[pl.ds(base + i, 4 * z4), :] = jnp.where(first, g[:, :HC], g[:, HC:])
            sent = jnp.where(first, g[:, HC:], g[:, :HC]).astype(bf16)
            for bb in range(4):
                rows = pl.ds(base + bb * 4 * z4 + i // 4, z4)
                send[rows, :] = sent[bb * z4 : (bb + 1) * z4]

        unrolled(H, 4 * z4, go)

    four_rows(2 * H, hn_t, cot_out, n_keep, n_r0s)
    n_rep = remote(n_r0s, n_r0, n_ss.at[0], n_rs.at[0], partner)
    n_rep.start()
    own[...] = mm(amat_t[:R, :], cot_g[...])
    csp[...] = nt(cot_pre[...], nw1[:H, :])
    s4_t[...] = nt(p4[...], st[...]).astype(bf16)

    QC = HC // 2

    def add_partner(parts, keep, got, send):
        def go(i):
            for aa in range(4):
                off = 0
                for base, size in parts:
                    step = size // 4
                    rows = pl.ds(pl.multiple_of(base + aa * size + i * step, step), step)
                    total = (keep[rows, :] + got[rows, :].astype(f32)).astype(bf16)
                    there = pl.ds(pl.multiple_of(off + i * step, step), step)
                    send[0, aa, there, :] = total[:, :QC]
                    send[1, aa, there, :] = total[:, QC:]
                    off += size

        lax.fori_loop(0, 4, lambda i, c: (go(i), c)[1], 0)

    def first_step(send, recv, ss, rs):
        copies = []
        for half, near in ((0, a1), (1, a3)):
            for slot, chunk in ((1, a2), (0, near)):
                k = 1 + 2 * half + slot
                copies.append(
                    remote(send.at[half, chunk], recv.at[half, slot], ss.at[k], rs.at[k], a_at(near))
                )
        for copy in copies:
            copy.start()
        return copies

    def second_step(copies, send, recv, mid_s, mid_r, ss, rs):
        for copy in copies:
            copy.wait_recv()
        more = []
        for half, near in ((0, a3), (1, a1)):
            mid_s[half] = (send[half, near].astype(f32) + recv[half, 1].astype(f32)).astype(bf16)
            k = 5 + half
            copy = remote(mid_s.at[half], mid_r.at[half], ss.at[k], rs.at[k], a_at(near))
            copy.start()
            more.append(copy)
        return more

    def b_stage(copies, send, recv, mid_r, out, got, parts, ss, rs):
        for copy in copies:
            copy.wait_recv()
        for bb in range(4):
            lo = 0
            off = 0
            for size in parts:
                rows = pl.ds(lo + bb * (size // 4), size // 4)
                halves = [
                    send[h, a, rows, :].astype(f32) + recv[h, 0, rows, :].astype(f32) + mid_r[h, rows, :].astype(f32)
                    for h in range(2)
                ]
                out[bb, off : off + size // 4, :] = jnp.concatenate(halves, axis=1).astype(bf16)
                lo += size
                off += size // 4
        more = [
            remote(out.at[(b + j) % 4], got.at[j - 1], ss.at[6 + j], rs.at[6 + j], b_peer(j)) for j in (2, 1, 3)
        ]
        for copy in more:
            copy.start()
        return more

    def b_sum(copies, send, recv):
        for copy in copies:
            copy.wait_recv()
        total = send[b].astype(f32)
        for j in range(3):
            total = total + recv[j].astype(f32)
        return total

    n_parts, e_parts = ((0, 2 * H // 4), (2 * H, H // 4)), ((0, H // 4),)
    n_sizes, e_sizes = (2 * H // 4, H // 4), (H // 4,)
    k8 = 2 * K4

    n_rep.wait_recv()
    add_partner(n_parts, n_keep, n_r0, n_s1s)
    n1 = first_step(n_s1s, n_s1, n_ss, n_rs)

    for j in range(4):

        @pl.when(has[j])
        def _():
            home[back[j]].wait_recv()

    def fold(i):
        rows = pl.ds(i, CH)
        for blk in range(BLK):
            full = pl.ds(blk * B + i, CH)
            total = own[full, :]
            for j in range(4):
                total = total + jnp.where(snd_s[0, j] == blk, ret[j, rows, :].astype(f32), 0.0)
            cot_msg[full, :] = total.astype(bf16)

    unrolled(B, CH, fold)

    four_rows(0, he_t, cot_msg, u_keep, u_r0s)
    u_rep = remote(u_r0s, u_r0, u_ss.at[0], u_rs.at[0], partner)
    u_rep.start()
    n2 = second_step(n1, n_s1s, n_s1, n_ts, n_t, n_ss, n_rs)
    tmp[...] = nt(cot_msg[...], ew2[...])

    def edge_slope(i):
        rows = pl.ds(i, CH)
        cot_pre_e[rows, :] = (tmp[rows, :] * slope[rows, :]).astype(bf16)

    unrolled(R, CH, edge_slope)
    four_rows(0, s4_t, cot_pre_e, v_keep, v_r0s)
    v_rep = remote(v_r0s, v_r0, v_ss.at[0], v_rs.at[0], partner)
    v_rep.start()
    u_rep.wait_recv()
    add_partner(e_parts, u_keep, u_r0, u_s1s)
    u1 = first_step(u_s1s, u_s1, u_ss, u_rs)

    csp[...] += nt(cot_pre_e[...], ew1[...])

    def finish_state(i):
        rows = pl.ds(i, CH)
        ct[rows, :] = (ct[rows, :].astype(f32) + csp[rows, :]).astype(bf16)

    unrolled(R, CH, finish_state)
    out_sg = pltpu.make_async_copy(ct, states_h.at[1], out_sem.at[1])
    out_sg.start()

    v_rep.wait_recv()
    add_partner(e_parts, v_keep, v_r0, v_s1s)
    v1 = first_step(v_s1s, v_s1, v_ss, v_rs)

    n3 = b_stage(n2, n_s1s, n_s1, n_t, n_s2s, n_s2, n_sizes, n_ss, n_rs)
    u2 = second_step(u1, u_s1s, u_s1, u_ts, u_t, u_ss, u_rs)
    v2 = second_step(v1, v_s1s, v_s1, v_ts, v_t, v_ss, v_rs)
    u3 = b_stage(u2, u_s1s, u_s1, u_t, u_s2s, u_s2, e_sizes, u_ss, u_rs)
    v3 = b_stage(v2, v_s1s, v_s1, v_t, v_s2s, v_s2, e_sizes, v_ss, v_rs)

    rows_n = b_sum(n3, n_s2s, n_s2)
    for zz in range(Z):
        pair = z8 + (zz // 2) * k8
        n_s3s[zz] = jnp.concatenate([rows_n[zz * k8 : (zz + 1) * k8], rows_n[pair : pair + k8]], axis=0).astype(bf16)
    n4 = []
    for j in range(1, Z):
        k = 9 + j
        n4.append(remote(n_s3s.at[(z + j) % Z], n_s3.at[j - 1], n_ss.at[k], n_rs.at[k], z_peer(j)))
    for copy in n4:
        copy.start()
    rows_u = b_sum(u3, u_s2s, u_s2)
    rows_v = b_sum(v3, v_s2s, v_s2)
    for zz in range(Z):
        e_s3s[zz] = jnp.concatenate(
            [rows_v[zz * K4 : (zz + 1) * K4], rows_u[zz * K4 : (zz + 1) * K4]], axis=0
        ).astype(bf16)
    e4 = []
    for j in range(1, Z):
        e4.append(remote(e_s3s.at[(z + j) % Z], e_s3.at[0, j], e_ss.at[j], e_rs.at[j], z_peer(j)))
    for j in range(Z):
        e4.append(remote(e_s3s.at[(z + j) % Z], e_s3.at[1, j], e_ss.at[Z + j], e_rs.at[Z + j], across(j)))
    for copy in e4:
        copy.start()

    def whole(mine, theirs):
        return jnp.concatenate([jnp.where(first, mine, theirs), jnp.where(first, theirs, mine)], axis=1)

    for copy in n4:
        copy.wait_recv()
    total = n_s3s[z].astype(f32)
    for j in range(Z - 1):
        total = total + n_s3[j].astype(f32)
    n_fs[...] = total
    n_fin = remote(n_fs, n_f, n_ss.at[9 + Z], n_rs.at[9 + Z], partner)
    n_fin.start()
    n_fin.wait_recv()
    full = whole(n_fs[...], n_f[...])
    grads[:k8, :] = full[:k8]
    grads[k8 : k8 + K4, :] = jnp.where(z % 2 == 1, full[k8 + K4 :], full[k8 : k8 + K4])
    for copy in e4:
        copy.wait_recv()
    mine, theirs = e_s3s[z].astype(f32), e_s3[1, 0].astype(f32)
    for j in range(1, Z):
        mine = mine + e_s3[0, j].astype(f32)
        theirs = theirs + e_s3[1, j].astype(f32)
    grads[2 * k8 :, :] = whole(mine, theirs)

    out_fs.wait()
    out_sg.wait()
    for j in range(4):

        @pl.when(has[j])
        def _():
            halo[j].wait_send()
            home[j].wait_send()

    for copy in [n_rep, u_rep, v_rep, n_fin] + n1 + n2 + n3 + n4 + u1 + u2 + u3 + v1 + v2 + v3 + e4:
        copy.wait_send()


def deliver(K4, states, grads, fs_h, sg_h, ge1_h, ge2_h, gn1_h, gn2_h, ge1, ge2, gn1, gn2, sem):
    out = [pltpu.make_async_copy(states.at[i], ref, sem.at[i]) for i, ref in enumerate((fs_h, sg_h))]
    for copy in out:
        copy.start()
    gn1[...] = grads[: 2 * K4, :]
    gn2[...] = grads[2 * K4 : 3 * K4, :]
    ge1[...] = grads[4 * K4 : 5 * K4, :]
    ge2[...] = grads[5 * K4 :, :]
    for i, (src, dst) in enumerate(((gn1, gn1_h), (gn2, gn2_h), (ge1, ge1_h), (ge2, ge2_h))):
        copy = pltpu.make_async_copy(src, dst, sem.at[2 + i])
        copy.start()
        out.append(copy)
    for copy in out:
        copy.wait()


def make_body(Z, X):
    def body(
        node_state, node_cot, edge_w1, edge_b1, edge_w2, node_w1, node_b1, node_w2, norm_gain,
        tile_dst, tile_src, tile_count, tile_vals, send_blocks,
    ):
        R, H = node_state.shape[3:]
        T, B = tile_vals.shape[2:4]
        Y = Y_LO * Y_HI
        HC = H // 2
        K4 = H // (Z * X * Y)
        k8 = 2 * K4

        def v(shape, dtype=bf16):
            return pltpu.VMEM(shape, dtype)

        def stages(total, s1, s2):
            return [
                v((total, HC), f32), v((total, HC)), v((total, HC)),
                v((2, 4, s1, HC // 2)), v((2, 2, s1, HC // 2)), v((2, s1, HC // 2)), v((2, s1, HC // 2)),
                v((4, s2, HC)), v((3, s2, HC)),
            ]

        dma = pltpu.SemaphoreType.DMA
        scratch = [pltpu.SMEM((1, T), i32), pltpu.SMEM((1, T), i32), pltpu.SMEM((1, 1), i32), pltpu.SMEM((1, 4), i32)]
        scratch += [v((1, H), f32)] * 3
        scratch += [
            v((R, H)), v((R, H)), v((H, H)), v((H, H)), v((2 * H, H)), v((H, H)), v((T, B, B)), dma((14,)),
            v((R, H), f32), v((R, H)), v((BLK, B, H)), v((4, B, H)), v((4, B, H)), v((T, BLK * EXTENT, 16, B)),
            v((R, EXTENT * B)), v((EXTENT * B, R)), v((H, H)), v((H, H)),
            v((H, R)), v((H, R)), v((H, R)), v((H, R)), v((H, R)), v((R, H), f32), v((R, H)), v((R, H)), v((R, H)),
            v((R, H)), v((R, H), f32), v((R, H), f32), v((R, H), f32), v((R, H)),
            v((4, B, H)), v((4, B, H)), v((R, H)), v((R, H)),
        ]
        scratch += stages(3 * H, 3 * H // 4, 3 * H // 16)
        scratch += [v((Z, 2 * k8, HC)), v((Z - 1, 2 * k8, HC)), v((2 * k8, HC), f32), v((2 * k8, HC), f32)]
        scratch += stages(H, H // 4, H // 16) * 2
        scratch += [v((Z, k8, HC)), v((2, Z, k8, HC))]
        scratch += [dma((4,))] * 4 + [dma((10 + Z,))] * 2 + [dma((10,))] * 4 + [dma((2 * Z,))] * 2 + [dma((2,))]
        vmem = pl.BlockSpec(memory_space=pltpu.VMEM)
        hbm = pl.BlockSpec(memory_space=pltpu.HBM)
        anywhere = pl.BlockSpec(memory_space=pl.ANY)
        inputs = (
            tile_dst.reshape(1, T), tile_src.reshape(1, T), tile_count, send_blocks.reshape(1, 4),
            edge_b1.reshape(1, H), node_b1.reshape(1, H), norm_gain.reshape(1, H),
            node_state.reshape(R, H), node_cot.reshape(R, H), edge_w1.reshape(H, H), edge_w2.reshape(H, H),
            node_w1.reshape(2 * H, H), node_w2.reshape(H, H), tile_vals.reshape(T, B, B),
        )
        inputs = [
            array if i == 2 else pltpu.with_memory_space_constraint(array, pltpu.HBM) for i, array in enumerate(inputs)
        ]
        states, grads = pl.pallas_call(
            functools.partial(kernel, Z, X, H, B, T),
            out_shape=(jax.ShapeDtypeStruct((2, R, H), bf16), jax.ShapeDtypeStruct((6 * K4, H), f32)),
            in_specs=[hbm] * 14,
            out_specs=(anywhere, vmem),
            scratch_shapes=scratch,
            compiler_params=pltpu.CompilerParams(
                collective_id=0, has_side_effects=True, vmem_limit_bytes=40 * 1024 * 1024
            ),
            name="step",
        )(
            *inputs
        )
        outs = pl.pallas_call(
            functools.partial(deliver, K4),
            out_shape=(
                jax.ShapeDtypeStruct((R, H), bf16),
                jax.ShapeDtypeStruct((R, H), bf16),
                jax.ShapeDtypeStruct((K4, H), f32),
                jax.ShapeDtypeStruct((K4, H), f32),
                jax.ShapeDtypeStruct((k8, H), f32),
                jax.ShapeDtypeStruct((K4, H), f32),
            ),
            in_specs=[anywhere, vmem],
            out_specs=[hbm] * 6,
            scratch_shapes=[v((rows, H), f32) for rows in (K4, K4, k8, K4)] + [dma((6,))],
            compiler_params=pltpu.CompilerParams(vmem_limit_bytes=4 * 1024 * 1024),
            name="deliver",
        )(states, grads)
        return (outs[0].reshape(node_state.shape), outs[1].reshape(node_state.shape)) + tuple(outs[2:])

    return body


def solution(mesh):
    in_specs = (
        P("rep", "stream", "span", None, None),
        P("rep", "stream", "span", None, None),
        P(), P(), P(), P(), P(), P(), P(),
        P("stream", "span", None),
        P("stream", "span", None),
        P("stream", "span"),
        P("stream", "span", None, None, None),
        P("stream", "span", None, None),
    )
    out_specs = (
        P("rep", "stream", "span", None, None),
        P("rep", "stream", "span", None, None),
        P(("stream", "span"), None),
        P(("stream", "span"), None),
        P(("stream", "span"), None),
        P(("stream", "span"), None),
    )
    body = make_body(mesh.shape["stream"] // Y_LO, mesh.shape["span"] // Y_HI)
    return jax.shard_map(body, mesh=mesh, in_specs=in_specs, out_specs=out_specs, check_vma=False)
```

```python
import functools

import jax
import jax.numpy as jnp
from jax import lax
from jax.experimental import pallas as pl
from jax.experimental.pallas import tpu as pltpu
from jax.sharding import PartitionSpec as P

norm_epsilon = 1e-05
f32, bf16, i32 = jnp.float32, jnp.bfloat16, jnp.int32
MESH = pl.DeviceIdType.MESH
Y_LO = 2
Y_HI = 2
BLK = 3
EXTENT = 7


def log2(n):
    assert n & (n - 1) == 0
    return n.bit_length() - 1


def mm(left_op, right_op):
    return jnp.dot(left_op, right_op, preferred_element_type=f32)


def nt(left_op, right_op):
    return lax.dot_general(left_op, right_op, (((1,), (1,)), ((), ())), preferred_element_type=f32)


def unrolled(total, step, fn):
    for i in range(0, total, step):
        fn(i)


def loop(total, step, fn):
    def trip(i, carry):
        fn(pl.multiple_of(i * step, step))
        return carry

    lax.fori_loop(0, total // step, trip, 0)


def kernel(
    Z, X, H, B, T,
    dst_h, src_h, cnt_h, snd_h, eb1_h, nb1_h, gain_h,
    st_h, ct_h, ew1_h, ew2_h, nw1_h, nw2_h, vals_h,
    states_h, grads,
    dst_s, src_s, cnt_s, snd_s, eb1, nb1, gain,
    st, ct, ew1, ew2, nw1, nw2, vals, in_sem,
    slope, hid, msg, ext, sendb, mask, amat, amat_t, p4, p8,
    he_t, s4_t, s8_t, g8_t, hn_t, part, gath, cot_out, cot_pre, cot_g, csp, own, tmp, fsv,
    rets, ret, cot_msg, cot_pre_e,
    n_keep, n_r0s, n_r0, n_s1s, n_s1, n_ts, n_t, n_s2s, n_s2, n_s3s, n_s3, n_fs, n_f,
    u_keep, u_r0s, u_r0, u_s1s, u_s1, u_ts, u_t, u_s2s, u_s2,
    v_keep, v_r0s, v_r0, v_s1s, v_s1, v_ts, v_t, v_s2s, v_s2,
    e_s3s, e_s3,
    halo_ss, halo_rs, ret_ss, ret_rs, n_ss, n_rs, u_ss, u_rs, v_ss, v_rs, e_ss, e_rs, out_sem,
):
    R = BLK * B
    HC = H // 2
    Y = Y_LO * Y_HI
    SHARDS = Z * X * Y
    K4 = H // SHARDS
    s = lax.axis_index("stream")
    p = lax.axis_index("span")
    r = lax.axis_index("rep")
    y_lo, z = s // Z, s % Z
    y_hi, x = p // X, p % X
    y = y_hi * Y_LO + y_lo
    first = r == 0
    a = jnp.where(first, y, x)
    b = jnp.where(first, x, y)
    has = (s > 0, s < Y_LO * Z - 1, p > 0, p < Y_HI * X - 1)

    def at(yy, xx, zz):
        return {"stream": (yy % Y_LO) * Z + zz, "span": (yy // Y_LO) * X + xx, "rep": r}

    a1, a3 = a + 1 - 2 * (a % 2), 3 - a
    a2 = (a + 2) % 4

    def a_at(aa):
        return at(jnp.where(first, aa, y), jnp.where(first, x, aa), z)

    def b_peer(j):
        return at(jnp.where(first, y, (y + j) % Y), jnp.where(first, (x + j) % X, x), z)

    def z_peer(j):
        return at(y, x, (z + j) % Z)

    def across(j):
        return {**z_peer(j), "rep": 1 - r}

    partner = {"stream": s, "span": p, "rep": 1 - r}
    sides = (
        {"stream": s - 1, "span": p, "rep": r},
        {"stream": s + 1, "span": p, "rep": r},
        {"stream": s, "span": p - 1, "rep": r},
        {"stream": s, "span": p + 1, "rep": r},
    )

    def remote(src, dst, ssem, rsem, dev):
        return pltpu.make_async_remote_copy(
            src_ref=src, dst_ref=dst, send_sem=ssem, recv_sem=rsem, device_id=dev, device_id_type=MESH
        )

    pairs = (
        (st_h, st), (ew1_h, ew1), (eb1_h, eb1), (snd_h, snd_s), (ew2_h, ew2),
        (dst_h, dst_s), (src_h, src_s), (cnt_h, cnt_s), (vals_h, vals),
        (nw1_h, nw1), (nb1_h, nb1), (nw2_h, nw2), (ct_h, ct), (gain_h, gain),
    )
    loads = [pltpu.make_async_copy(src, dst, in_sem.at[i]) for i, (src, dst) in enumerate(pairs)]
    for copy in loads[:5]:
        copy.start()

    def load(*which):
        for i in which:
            loads[i].wait()

    barrier = pltpu.get_barrier_semaphore()
    peers = [a_at(a1), a_at(a3)] + [b_peer(j) for j in range(1, 4)]
    peers += [z_peer(j) for j in range(1, Z)] + [across(j) for j in range(Z)]
    for dev in peers:
        pl.semaphore_signal(barrier, inc=1, device_id=dev, device_id_type=MESH)
    halo_count = 0
    for side in range(4):
        halo_count = halo_count + has[side].astype(i32)

        @pl.when(has[side])
        def _():
            pl.semaphore_signal(barrier, inc=1, device_id=sides[side], device_id_type=MESH)

    CH = min(32, B)
    load(0, 1, 2)
    for copy in loads[5:]:
        copy.start()
    tmp[...] = mm(st[...], ew1[...])

    def edge_act(i):
        rows = pl.ds(i, CH)
        pre = tmp[rows, :] + eb1[...]
        g = jax.nn.sigmoid(pre)
        hid[rows, :] = (pre * g).astype(bf16)
        slope[rows, :] = pre

    unrolled(R, CH, edge_act)
    load(3, 4)
    tmp[...] = mm(hid[...], ew2[...])
    for blk in range(BLK):
        msg[blk] = tmp[blk * B : (blk + 1) * B, :].astype(bf16)
    for j in range(4):
        sendb[j] = msg[snd_s[0, j]]
    pl.semaphore_wait(barrier, len(peers) + halo_count)

    back = (1, 0, 3, 2)
    halo = [
        remote(sendb.at[j], ext.at[back[j]], halo_ss.at[j], halo_rs.at[back[j]], sides[j]) for j in range(4)
    ]
    for j in range(4):

        @pl.when(has[j])
        def _():
            halo[j].start()

        @pl.when(jnp.logical_not(has[j]))
        def _():
            ext[j] = jnp.zeros((B, H), bf16)
            ret[j] = jnp.zeros((B, H), bf16)

    def masks(t, carry):
        key = jnp.where(t < cnt_s[0, 0], dst_s[0, t] * EXTENT + src_s[0, t], -1)
        keys = jnp.full((16, B), key, i32)
        for q in range(BLK * EXTENT):
            mask[t, q] = jnp.where(keys == q, 1.0, 0.0).astype(bf16)
        return carry

    load(5, 6, 7)
    lax.fori_loop(0, T, masks, 0)
    load(8)

    def tiles(i):
        rows = pl.ds(i, CH)
        totals = [jnp.zeros((CH, B), bf16)] * (BLK * EXTENT)
        for t in range(T):
            v = vals[t, rows, :]
            totals = [
                total + jnp.concatenate([mask[t, q]] * (CH // 16), axis=0) * v for q, total in enumerate(totals)
            ]
        for q, total in enumerate(totals):
            d, e = q // EXTENT, q % EXTENT
            amat[pl.ds(pl.multiple_of(d * B + i, CH), CH), e * B : (e + 1) * B] = total

    loop(B, CH, tiles)
    eye = (lax.broadcasted_iota(i32, (B, B), 0) == lax.broadcasted_iota(i32, (B, B), 1)).astype(f32).astype(bf16)
    for e in range(EXTENT):
        amat_t[e * B : (e + 1) * B, :] = nt(eye, amat[:, e * B : (e + 1) * B]).astype(bf16)

    lk, lz = log2(K4), log2(Z)
    LW = min(128, H)

    def perms(i):
        pos = i + lax.broadcasted_iota(i32, (CH, LW), 0)
        lane = lax.broadcasted_iota(i32, (CH, LW), 1)
        zz = (pos >> lk) & (Z - 1)
        bb = (pos >> (lk + lz)) & 3
        aa = (pos >> (lk + lz + 2)) & 3
        yy, xx = jnp.where(first, aa, bb), jnp.where(first, bb, aa)
        four = (((yy & 1) * Z + zz) * Y_HI + (yy >> 1)) * (X * K4) + xx * K4 + (pos & (K4 - 1))
        zz = (pos >> (lk + 1)) & (Z - 1)
        q = (pos >> (lk + 1 + lz)) & (2 * X - 1)
        yh, xx = jnp.where(first, q >> 2, q & 1), jnp.where(first, q & 3, q >> 1)
        eight = (zz * Y_HI + yh) * (2 * X * K4) + xx * (2 * K4) + (pos & (2 * K4 - 1))
        rows = pl.ds(i, CH)
        for ref, orig in ((p4, four), (p8, eight)):
            for c in range(H // LW):
                ref[rows, c * LW : (c + 1) * LW] = jnp.where(orig == lane + c * LW, 1.0, 0.0).astype(bf16)

    loop(H, CH, perms)
    def to_slope(i):
        rows = pl.ds(i, CH)
        pre = slope[rows, :]
        g = jax.nn.sigmoid(pre)
        slope[rows, :] = g * (1.0 + pre * (1.0 - g))

    unrolled(R, CH, to_slope)
    he_t[...] = nt(p4[...], hid[...]).astype(bf16)
    s8_t[...] = nt(p8[...], st[...]).astype(bf16)
    load(9, 10)
    part[...] = mm(st[...], nw1[:H, :])
    own[...] = mm(amat[:, :R], msg[...].reshape(R, H))
    load(11, 12, 13)

    for j in range(4):

        @pl.when(has[j])
        def _():
            halo[back[j]].wait_recv()

    gath[...] = (own[...] + mm(amat[:, R:], ext[...].reshape(4 * B, H))).astype(bf16)
    part[...] += mm(gath[...], nw1[H:, :])

    def node_act(i):
        rows = pl.ds(i, CH)
        pre = part[rows, :] + nb1[...]
        g = jax.nn.sigmoid(pre)
        hid[rows, :] = (pre * g).astype(bf16)
        part[rows, :] = g * (1.0 + pre * (1.0 - g))

    unrolled(R, CH, node_act)
    tmp[...] = mm(hid[...], nw2[...])

    def norm(i):
        rows = pl.ds(i, CH)
        o = tmp[rows, :]
        centred = o - jnp.mean(o, axis=1, keepdims=True)
        inv = lax.rsqrt(jnp.mean(centred * centred, axis=1, keepdims=True) + norm_epsilon)
        normed = centred * inv
        fsv[rows, :] = (st[rows, :].astype(f32) + normed * gain[...]).astype(bf16)
        q = ct[rows, :].astype(f32) * gain[...]
        cot = inv * (
            q - jnp.mean(q, axis=1, keepdims=True) - normed * jnp.mean(q * normed, axis=1, keepdims=True)
        )
        cot_out[rows, :] = cot.astype(bf16)

    unrolled(R, CH, norm)
    out_fs = pltpu.make_async_copy(fsv, states_h.at[0], out_sem.at[0])
    out_fs.start()
    tmp[...] = nt(cot_out[...], nw2[...])

    def node_slope(i):
        rows = pl.ds(i, CH)
        cot_pre[rows, :] = (tmp[rows, :] * part[rows, :]).astype(bf16)

    unrolled(R, CH, node_slope)
    cot_g[...] = nt(cot_pre[...], nw1[H:, :]).astype(bf16)

    rets[...] = mm(amat_t[R:, :], cot_g[...]).astype(bf16).reshape(4, B, H)
    home = [
        remote(rets.at[g], ret.at[back[g]], ret_ss.at[g], ret_rs.at[back[g]], sides[g]) for g in range(4)
    ]
    for g in range(4):

        @pl.when(has[g])
        def _():
            home[g].start()

    hn_t[...] = nt(p4[...], hid[...]).astype(bf16)
    g8_t[...] = nt(p8[...], gath[...]).astype(bf16)
    z8, z4 = 2 * K4 * Z, K4 * Z

    def n1_grad(i):
        for y_low, left in ((0, s8_t), (1, g8_t)):
            g = mm(left[pl.ds(i, 2 * z8), :], cot_pre[...])
            sent = jnp.where(first, g[:, HC:], g[:, :HC]).astype(bf16)
            kept = jnp.where(first, g[:, :HC], g[:, HC:])
            for half in range(2):
                q = i // z8 + half
                yy = jnp.where(first, q // 4, q % 2) * 2 + y_low
                xx = jnp.where(first, q % 4, q // 2)
                aa, bb = jnp.where(first, yy, xx), jnp.where(first, xx, yy)
                block = slice(half * z8, (half + 1) * z8)
                n_keep[pl.ds(pl.multiple_of((aa * 4 + bb) * z8, z8), z8), :] = kept[block]
                n_r0s[pl.ds(pl.multiple_of((bb * 4 + aa) * z8, z8), z8), :] = sent[block]

    unrolled(H, 2 * z8, n1_grad)

    def four_rows(base, left, right, keep, send):
        def go(i):
            g = mm(left[pl.ds(i, 4 * z4), :], right[...])
            keep[pl.ds(base + i, 4 * z4), :] = jnp.where(first, g[:, :HC], g[:, HC:])
            sent = jnp.where(first, g[:, HC:], g[:, :HC]).astype(bf16)
            for bb in range(4):
                rows = pl.ds(base + bb * 4 * z4 + i // 4, z4)
                send[rows, :] = sent[bb * z4 : (bb + 1) * z4]

        unrolled(H, 4 * z4, go)

    four_rows(2 * H, hn_t, cot_out, n_keep, n_r0s)
    n_rep = remote(n_r0s, n_r0, n_ss.at[0], n_rs.at[0], partner)
    n_rep.start()
    own[...] = mm(amat_t[:R, :], cot_g[...])
    csp[...] = nt(cot_pre[...], nw1[:H, :])
    s4_t[...] = nt(p4[...], st[...]).astype(bf16)

    QC = HC // 2

    def add_partner(parts, keep, got, send):
        def go(i):
            for aa in range(4):
                off = 0
                for base, size in parts:
                    step = size // 4
                    rows = pl.ds(pl.multiple_of(base + aa * size + i * step, step), step)
                    total = (keep[rows, :] + got[rows, :].astype(f32)).astype(bf16)
                    there = pl.ds(pl.multiple_of(off + i * step, step), step)
                    send[0, aa, there, :] = total[:, :QC]
                    send[1, aa, there, :] = total[:, QC:]
                    off += size

        lax.fori_loop(0, 4, lambda i, c: (go(i), c)[1], 0)

    def first_step(send, recv, ss, rs):
        copies = []
        for half, near in ((0, a1), (1, a3)):
            for slot, chunk in ((1, a2), (0, near)):
                k = 1 + 2 * half + slot
                copies.append(
                    remote(send.at[half, chunk], recv.at[half, slot], ss.at[k], rs.at[k], a_at(near))
                )
        for copy in copies:
            copy.start()
        return copies

    def second_step(copies, send, recv, mid_s, mid_r, ss, rs):
        for copy in copies:
            copy.wait_recv()
        more = []
        for half, near in ((0, a3), (1, a1)):
            mid_s[half] = (send[half, near].astype(f32) + recv[half, 1].astype(f32)).astype(bf16)
            k = 5 + half
            copy = remote(mid_s.at[half], mid_r.at[half], ss.at[k], rs.at[k], a_at(near))
            copy.start()
            more.append(copy)
        return more

    def b_stage(copies, send, recv, mid_r, out, got, parts, ss, rs):
        for copy in copies:
            copy.wait_recv()
        for bb in range(4):
            lo = 0
            off = 0
            for size in parts:
                rows = pl.ds(lo + bb * (size // 4), size // 4)
                halves = [
                    send[h, a, rows, :].astype(f32) + recv[h, 0, rows, :].astype(f32) + mid_r[h, rows, :].astype(f32)
                    for h in range(2)
                ]
                out[bb, off : off + size // 4, :] = jnp.concatenate(halves, axis=1).astype(bf16)
                lo += size
                off += size // 4
        more = [
            remote(out.at[(b + j) % 4], got.at[j - 1], ss.at[6 + j], rs.at[6 + j], b_peer(j)) for j in (2, 1, 3)
        ]
        for copy in more:
            copy.start()
        return more

    def b_sum(copies, send, recv):
        for copy in copies:
            copy.wait_recv()
        total = send[b].astype(f32)
        for j in range(3):
            total = total + recv[j].astype(f32)
        return total

    n_parts, e_parts = ((0, 2 * H // 4), (2 * H, H // 4)), ((0, H // 4),)
    n_sizes, e_sizes = (2 * H // 4, H // 4), (H // 4,)
    k8 = 2 * K4

    n_rep.wait_recv()
    add_partner(n_parts, n_keep, n_r0, n_s1s)

    for j in range(4):

        @pl.when(has[j])
        def _():
            home[back[j]].wait_recv()

    n1 = first_step(n_s1s, n_s1, n_ss, n_rs)

    def fold(i):
        rows = pl.ds(i, CH)
        for blk in range(BLK):
            full = pl.ds(blk * B + i, CH)
            total = own[full, :]
            for j in range(4):
                total = total + jnp.where(snd_s[0, j] == blk, ret[j, rows, :].astype(f32), 0.0)
            cot_msg[full, :] = total.astype(bf16)

    unrolled(B, CH, fold)

    four_rows(0, he_t, cot_msg, u_keep, u_r0s)
    u_rep = remote(u_r0s, u_r0, u_ss.at[0], u_rs.at[0], partner)
    u_rep.start()
    tmp[...] = nt(cot_msg[...], ew2[...])

    def edge_slope(i):
        rows = pl.ds(i, CH)
        cot_pre_e[rows, :] = (tmp[rows, :] * slope[rows, :]).astype(bf16)

    unrolled(R, CH, edge_slope)
    four_rows(0, s4_t, cot_pre_e, v_keep, v_r0s)
    v_rep = remote(v_r0s, v_r0, v_ss.at[0], v_rs.at[0], partner)
    v_rep.start()
    u_rep.wait_recv()
    add_partner(e_parts, u_keep, u_r0, u_s1s)
    u1 = first_step(u_s1s, u_s1, u_ss, u_rs)

    csp[...] += nt(cot_pre_e[...], ew1[...])

    def finish_state(i):
        rows = pl.ds(i, CH)
        ct[rows, :] = (ct[rows, :].astype(f32) + csp[rows, :]).astype(bf16)

    unrolled(R, CH, finish_state)
    out_sg = pltpu.make_async_copy(ct, states_h.at[1], out_sem.at[1])
    out_sg.start()

    v_rep.wait_recv()
    add_partner(e_parts, v_keep, v_r0, v_s1s)
    v1 = first_step(v_s1s, v_s1, v_ss, v_rs)
    n2 = second_step(n1, n_s1s, n_s1, n_ts, n_t, n_ss, n_rs)
    u2 = second_step(u1, u_s1s, u_s1, u_ts, u_t, u_ss, u_rs)
    v2 = second_step(v1, v_s1s, v_s1, v_ts, v_t, v_ss, v_rs)
    n3 = b_stage(n2, n_s1s, n_s1, n_t, n_s2s, n_s2, n_sizes, n_ss, n_rs)
    u3 = b_stage(u2, u_s1s, u_s1, u_t, u_s2s, u_s2, e_sizes, u_ss, u_rs)
    v3 = b_stage(v2, v_s1s, v_s1, v_t, v_s2s, v_s2, e_sizes, v_ss, v_rs)

    rows_n = b_sum(n3, n_s2s, n_s2)
    for zz in range(Z):
        pair = z8 + (zz // 2) * k8
        n_s3s[zz] = jnp.concatenate([rows_n[zz * k8 : (zz + 1) * k8], rows_n[pair : pair + k8]], axis=0).astype(bf16)
    n4 = []
    for j in range(1, Z):
        k = 9 + j
        n4.append(remote(n_s3s.at[(z + j) % Z], n_s3.at[j - 1], n_ss.at[k], n_rs.at[k], z_peer(j)))
    for copy in n4:
        copy.start()
    rows_u = b_sum(u3, u_s2s, u_s2)
    rows_v = b_sum(v3, v_s2s, v_s2)
    for zz in range(Z):
        e_s3s[zz] = jnp.concatenate(
            [rows_v[zz * K4 : (zz + 1) * K4], rows_u[zz * K4 : (zz + 1) * K4]], axis=0
        ).astype(bf16)
    e4 = []
    for j in range(1, Z):
        e4.append(remote(e_s3s.at[(z + j) % Z], e_s3.at[0, j], e_ss.at[j], e_rs.at[j], z_peer(j)))
    for j in range(Z):
        e4.append(remote(e_s3s.at[(z + j) % Z], e_s3.at[1, j], e_ss.at[Z + j], e_rs.at[Z + j], across(j)))
    for copy in e4:
        copy.start()

    def whole(mine, theirs):
        return jnp.concatenate([jnp.where(first, mine, theirs), jnp.where(first, theirs, mine)], axis=1)

    for copy in n4:
        copy.wait_recv()
    total = n_s3s[z].astype(f32)
    for j in range(Z - 1):
        total = total + n_s3[j].astype(f32)
    n_fs[...] = total
    n_fin = remote(n_fs, n_f, n_ss.at[9 + Z], n_rs.at[9 + Z], partner)
    n_fin.start()
    n_fin.wait_recv()
    full = whole(n_fs[...], n_f[...])
    grads[:k8, :] = full[:k8]
    grads[k8 : k8 + K4, :] = jnp.where(z % 2 == 1, full[k8 + K4 :], full[k8 : k8 + K4])
    for copy in e4:
        copy.wait_recv()
    mine, theirs = e_s3s[z].astype(f32), e_s3[1, 0].astype(f32)
    for j in range(1, Z):
        mine = mine + e_s3[0, j].astype(f32)
        theirs = theirs + e_s3[1, j].astype(f32)
    grads[2 * k8 :, :] = whole(mine, theirs)

    out_fs.wait()
    out_sg.wait()
    for j in range(4):

        @pl.when(has[j])
        def _():
            halo[j].wait_send()
            home[j].wait_send()

    for copy in [n_rep, u_rep, v_rep, n_fin] + n1 + n2 + n3 + n4 + u1 + u2 + u3 + v1 + v2 + v3 + e4:
        copy.wait_send()


def deliver(K4, states, grads, fs_h, sg_h, ge1_h, ge2_h, gn1_h, gn2_h, ge1, ge2, gn1, gn2, sem):
    out = [pltpu.make_async_copy(states.at[i], ref, sem.at[i]) for i, ref in enumerate((fs_h, sg_h))]
    for copy in out:
        copy.start()
    gn1[...] = grads[: 2 * K4, :]
    gn2[...] = grads[2 * K4 : 3 * K4, :]
    ge1[...] = grads[4 * K4 : 5 * K4, :]
    ge2[...] = grads[5 * K4 :, :]
    for i, (src, dst) in enumerate(((gn1, gn1_h), (gn2, gn2_h), (ge1, ge1_h), (ge2, ge2_h))):
        copy = pltpu.make_async_copy(src, dst, sem.at[2 + i])
        copy.start()
        out.append(copy)
    for copy in out:
        copy.wait()


def make_body(Z, X):
    def body(
        node_state, node_cot, edge_w1, edge_b1, edge_w2, node_w1, node_b1, node_w2, norm_gain,
        tile_dst, tile_src, tile_count, tile_vals, send_blocks,
    ):
        R, H = node_state.shape[3:]
        T, B = tile_vals.shape[2:4]
        Y = Y_LO * Y_HI
        HC = H // 2
        K4 = H // (Z * X * Y)
        k8 = 2 * K4

        def v(shape, dtype=bf16):
            return pltpu.VMEM(shape, dtype)

        def stages(total, s1, s2):
            return [
                v((total, HC), f32), v((total, HC)), v((total, HC)),
                v((2, 4, s1, HC // 2)), v((2, 2, s1, HC // 2)), v((2, s1, HC // 2)), v((2, s1, HC // 2)),
                v((4, s2, HC)), v((3, s2, HC)),
            ]

        dma = pltpu.SemaphoreType.DMA
        scratch = [pltpu.SMEM((1, T), i32), pltpu.SMEM((1, T), i32), pltpu.SMEM((1, 1), i32), pltpu.SMEM((1, 4), i32)]
        scratch += [v((1, H), f32)] * 3
        scratch += [
            v((R, H)), v((R, H)), v((H, H)), v((H, H)), v((2 * H, H)), v((H, H)), v((T, B, B)), dma((14,)),
            v((R, H), f32), v((R, H)), v((BLK, B, H)), v((4, B, H)), v((4, B, H)), v((T, BLK * EXTENT, 16, B)),
            v((R, EXTENT * B)), v((EXTENT * B, R)), v((H, H)), v((H, H)),
            v((H, R)), v((H, R)), v((H, R)), v((H, R)), v((H, R)), v((R, H), f32), v((R, H)), v((R, H)), v((R, H)),
            v((R, H)), v((R, H), f32), v((R, H), f32), v((R, H), f32), v((R, H)),
            v((4, B, H)), v((4, B, H)), v((R, H)), v((R, H)),
        ]
        scratch += stages(3 * H, 3 * H // 4, 3 * H // 16)
        scratch += [v((Z, 2 * k8, HC)), v((Z - 1, 2 * k8, HC)), v((2 * k8, HC), f32), v((2 * k8, HC), f32)]
        scratch += stages(H, H // 4, H // 16) * 2
        scratch += [v((Z, k8, HC)), v((2, Z, k8, HC))]
        scratch += [dma((4,))] * 4 + [dma((10 + Z,))] * 2 + [dma((10,))] * 4 + [dma((2 * Z,))] * 2 + [dma((2,))]
        vmem = pl.BlockSpec(memory_space=pltpu.VMEM)
        hbm = pl.BlockSpec(memory_space=pltpu.HBM)
        anywhere = pl.BlockSpec(memory_space=pl.ANY)
        inputs = (
            tile_dst.reshape(1, T), tile_src.reshape(1, T), tile_count, send_blocks.reshape(1, 4),
            edge_b1.reshape(1, H), node_b1.reshape(1, H), norm_gain.reshape(1, H),
            node_state.reshape(R, H), node_cot.reshape(R, H), edge_w1.reshape(H, H), edge_w2.reshape(H, H),
            node_w1.reshape(2 * H, H), node_w2.reshape(H, H), tile_vals.reshape(T, B, B),
        )
        inputs = [
            array if i == 2 else pltpu.with_memory_space_constraint(array, pltpu.HBM) for i, array in enumerate(inputs)
        ]
        states, grads = pl.pallas_call(
            functools.partial(kernel, Z, X, H, B, T),
            out_shape=(jax.ShapeDtypeStruct((2, R, H), bf16), jax.ShapeDtypeStruct((6 * K4, H), f32)),
            in_specs=[hbm] * 14,
            out_specs=(anywhere, vmem),
            scratch_shapes=scratch,
            compiler_params=pltpu.CompilerParams(
                collective_id=0, has_side_effects=True, vmem_limit_bytes=40 * 1024 * 1024
            ),
            name="step",
        )(
            *inputs
        )
        outs = pl.pallas_call(
            functools.partial(deliver, K4),
            out_shape=(
                jax.ShapeDtypeStruct((R, H), bf16),
                jax.ShapeDtypeStruct((R, H), bf16),
                jax.ShapeDtypeStruct((K4, H), f32),
                jax.ShapeDtypeStruct((K4, H), f32),
                jax.ShapeDtypeStruct((k8, H), f32),
                jax.ShapeDtypeStruct((K4, H), f32),
            ),
            in_specs=[anywhere, vmem],
            out_specs=[hbm] * 6,
            scratch_shapes=[v((rows, H), f32) for rows in (K4, K4, k8, K4)] + [dma((6,))],
            compiler_params=pltpu.CompilerParams(vmem_limit_bytes=4 * 1024 * 1024),
            name="deliver",
        )(states, grads)
        return (outs[0].reshape(node_state.shape), outs[1].reshape(node_state.shape)) + tuple(outs[2:])

    return body


def solution(mesh):
    in_specs = (
        P("rep", "stream", "span", None, None),
        P("rep", "stream", "span", None, None),
        P(), P(), P(), P(), P(), P(), P(),
        P("stream", "span", None),
        P("stream", "span", None),
        P("stream", "span"),
        P("stream", "span", None, None, None),
        P("stream", "span", None, None),
    )
    out_specs = (
        P("rep", "stream", "span", None, None),
        P("rep", "stream", "span", None, None),
        P(("stream", "span"), None),
        P(("stream", "span"), None),
        P(("stream", "span"), None),
        P(("stream", "span"), None),
    )
    body = make_body(mesh.shape["stream"] // Y_LO, mesh.shape["span"] // Y_HI)
    return jax.shard_map(body, mesh=mesh, in_specs=in_specs, out_specs=out_specs, check_vma=False)
```

```python
import functools

import jax
import jax.numpy as jnp
from jax import lax
from jax.experimental import pallas as pl
from jax.experimental.pallas import tpu as pltpu
from jax.sharding import PartitionSpec as P

norm_epsilon = 1e-05
f32, bf16, i32 = jnp.float32, jnp.bfloat16, jnp.int32
MESH = pl.DeviceIdType.MESH
Y_LO = 2
Y_HI = 2
BLK = 3
EXTENT = 7


def log2(n):
    assert n & (n - 1) == 0
    return n.bit_length() - 1


def mm(left_op, right_op):
    return jnp.dot(left_op, right_op, preferred_element_type=f32)


def nt(left_op, right_op):
    return lax.dot_general(left_op, right_op, (((1,), (1,)), ((), ())), preferred_element_type=f32)


def unrolled(total, step, fn):
    for i in range(0, total, step):
        fn(i)


def loop(total, step, fn):
    def trip(i, carry):
        fn(pl.multiple_of(i * step, step))
        return carry

    lax.fori_loop(0, total // step, trip, 0)


def kernel(
    Z, X, H, B, T,
    dst_h, src_h, cnt_h, snd_h, eb1_h, nb1_h, gain_h,
    st_h, ct_h, ew1_h, ew2_h, nw1_h, nw2_h, vals_h,
    states_h, grads,
    dst_s, src_s, cnt_s, snd_s, eb1, nb1, gain,
    st, ct, ew1, ew2, nw1, nw2, vals, in_sem,
    slope, hid, msg, ext, sendb, mask, amat, amat_t, p4, p8,
    he_t, s4_t, s8_t, g8_t, hn_t, part, gath, cot_out, cot_pre, cot_g, csp, own, tmp, fsv,
    rets, ret, fsel, cot_msg, cot_pre_e,
    n_keep, n_r0s, n_r0, n_s1s, n_s1, n_ts, n_t, n_s2s, n_s2, n_s3s, n_s3, n_fs, n_f,
    u_keep, u_r0s, u_r0, u_s1s, u_s1, u_ts, u_t, u_s2s, u_s2,
    v_keep, v_r0s, v_r0, v_s1s, v_s1, v_ts, v_t, v_s2s, v_s2,
    e_s3s, e_s3,
    halo_ss, halo_rs, ret_ss, ret_rs, n_ss, n_rs, u_ss, u_rs, v_ss, v_rs, e_ss, e_rs, out_sem,
):
    R = BLK * B
    HC = H // 2
    Y = Y_LO * Y_HI
    SHARDS = Z * X * Y
    K4 = H // SHARDS
    s = lax.axis_index("stream")
    p = lax.axis_index("span")
    r = lax.axis_index("rep")
    y_lo, z = s // Z, s % Z
    y_hi, x = p // X, p % X
    y = y_hi * Y_LO + y_lo
    first = r == 0
    a = jnp.where(first, y, x)
    b = jnp.where(first, x, y)
    has = (s > 0, s < Y_LO * Z - 1, p > 0, p < Y_HI * X - 1)

    def at(yy, xx, zz):
        return {"stream": (yy % Y_LO) * Z + zz, "span": (yy // Y_LO) * X + xx, "rep": r}

    a1, a3 = a + 1 - 2 * (a % 2), 3 - a
    a2 = (a + 2) % 4

    def a_at(aa):
        return at(jnp.where(first, aa, y), jnp.where(first, x, aa), z)

    def b_peer(j):
        return at(jnp.where(first, y, (y + j) % Y), jnp.where(first, (x + j) % X, x), z)

    def z_peer(j):
        return at(y, x, (z + j) % Z)

    def across(j):
        return {**z_peer(j), "rep": 1 - r}

    partner = {"stream": s, "span": p, "rep": 1 - r}
    sides = (
        {"stream": s - 1, "span": p, "rep": r},
        {"stream": s + 1, "span": p, "rep": r},
        {"stream": s, "span": p - 1, "rep": r},
        {"stream": s, "span": p + 1, "rep": r},
    )

    def remote(src, dst, ssem, rsem, dev):
        return pltpu.make_async_remote_copy(
            src_ref=src, dst_ref=dst, send_sem=ssem, recv_sem=rsem, device_id=dev, device_id_type=MESH
        )

    pairs = (
        (st_h, st), (ew1_h, ew1), (eb1_h, eb1), (snd_h, snd_s), (ew2_h, ew2),
        (dst_h, dst_s), (src_h, src_s), (cnt_h, cnt_s), (vals_h, vals),
        (nw1_h, nw1), (nb1_h, nb1), (nw2_h, nw2), (ct_h, ct), (gain_h, gain),
    )
    loads = [pltpu.make_async_copy(src, dst, in_sem.at[i]) for i, (src, dst) in enumerate(pairs)]
    for copy in loads[:5]:
        copy.start()

    def load(*which):
        for i in which:
            loads[i].wait()

    barrier = pltpu.get_barrier_semaphore()
    peers = [a_at(a1), a_at(a3)] + [b_peer(j) for j in range(1, 4)]
    peers += [z_peer(j) for j in range(1, Z)] + [across(j) for j in range(Z)]
    for dev in peers:
        pl.semaphore_signal(barrier, inc=1, device_id=dev, device_id_type=MESH)
    halo_count = 0
    for side in range(4):
        halo_count = halo_count + has[side].astype(i32)

        @pl.when(has[side])
        def _():
            pl.semaphore_signal(barrier, inc=1, device_id=sides[side], device_id_type=MESH)

    CH = min(32, B)
    load(0, 1, 2)
    for copy in loads[5:]:
        copy.start()
    tmp[...] = mm(st[...], ew1[...])

    def edge_act(i):
        rows = pl.ds(i, CH)
        pre = tmp[rows, :] + eb1[...]
        g = jax.nn.sigmoid(pre)
        hid[rows, :] = (pre * g).astype(bf16)
        slope[rows, :] = pre

    unrolled(R, CH, edge_act)
    load(3, 4)
    tmp[...] = mm(hid[...], ew2[...])
    for blk in range(BLK):
        msg[blk] = tmp[blk * B : (blk + 1) * B, :].astype(bf16)
    for j in range(4):
        sendb[j] = msg[snd_s[0, j]]
    pl.semaphore_wait(barrier, len(peers) + halo_count)

    back = (1, 0, 3, 2)
    halo = [
        remote(sendb.at[j], ext.at[back[j]], halo_ss.at[j], halo_rs.at[back[j]], sides[j]) for j in range(4)
    ]
    for j in range(4):

        @pl.when(has[j])
        def _():
            halo[j].start()

        @pl.when(jnp.logical_not(has[j]))
        def _():
            ext[j] = jnp.zeros((B, H), bf16)
            ret[j] = jnp.zeros((B, H), bf16)

    def masks(t, carry):
        key = jnp.where(t < cnt_s[0, 0], dst_s[0, t] * EXTENT + src_s[0, t], -1)
        keys = jnp.full((16, B), key, i32)
        for q in range(BLK * EXTENT):
            mask[t, q] = jnp.where(keys == q, 1.0, 0.0).astype(bf16)
        return carry

    load(5, 6, 7)
    lax.fori_loop(0, T, masks, 0)
    load(8)

    def tiles(i):
        rows = pl.ds(i, CH)
        totals = [jnp.zeros((CH, B), bf16)] * (BLK * EXTENT)
        for t in range(T):
            v = vals[t, rows, :]
            totals = [
                total + jnp.concatenate([mask[t, q]] * (CH // 16), axis=0) * v for q, total in enumerate(totals)
            ]
        for q, total in enumerate(totals):
            d, e = q // EXTENT, q % EXTENT
            amat[pl.ds(pl.multiple_of(d * B + i, CH), CH), e * B : (e + 1) * B] = total

    loop(B, CH, tiles)
    eye = (lax.broadcasted_iota(i32, (B, B), 0) == lax.broadcasted_iota(i32, (B, B), 1)).astype(f32).astype(bf16)
    for e in range(EXTENT):
        amat_t[e * B : (e + 1) * B, :] = nt(eye, amat[:, e * B : (e + 1) * B]).astype(bf16)

    lk, lz = log2(K4), log2(Z)
    LW = min(128, H)

    def perms(i):
        pos = i + lax.broadcasted_iota(i32, (CH, LW), 0)
        lane = lax.broadcasted_iota(i32, (CH, LW), 1)
        zz = (pos >> lk) & (Z - 1)
        bb = (pos >> (lk + lz)) & 3
        aa = (pos >> (lk + lz + 2)) & 3
        yy, xx = jnp.where(first, aa, bb), jnp.where(first, bb, aa)
        four = (((yy & 1) * Z + zz) * Y_HI + (yy >> 1)) * (X * K4) + xx * K4 + (pos & (K4 - 1))
        zz = (pos >> (lk + 1)) & (Z - 1)
        q = (pos >> (lk + 1 + lz)) & (2 * X - 1)
        yh, xx = jnp.where(first, q >> 2, q & 1), jnp.where(first, q & 3, q >> 1)
        eight = (zz * Y_HI + yh) * (2 * X * K4) + xx * (2 * K4) + (pos & (2 * K4 - 1))
        rows = pl.ds(i, CH)
        for ref, orig in ((p4, four), (p8, eight)):
            for c in range(H // LW):
                ref[rows, c * LW : (c + 1) * LW] = jnp.where(orig == lane + c * LW, 1.0, 0.0).astype(bf16)

    loop(H, CH, perms)
    def to_slope(i):
        rows = pl.ds(i, CH)
        pre = slope[rows, :]
        g = jax.nn.sigmoid(pre)
        slope[rows, :] = g * (1.0 + pre * (1.0 - g))

    unrolled(R, CH, to_slope)
    he_t[...] = nt(p4[...], hid[...]).astype(bf16)
    s8_t[...] = nt(p8[...], st[...]).astype(bf16)
    load(9, 10)
    part[...] = mm(st[...], nw1[:H, :])
    own[...] = mm(amat[:, :R], msg[...].reshape(R, H))
    load(11, 12, 13)

    for j in range(4):

        @pl.when(has[j])
        def _():
            halo[back[j]].wait_recv()

    gath[...] = (own[...] + mm(amat[:, R:], ext[...].reshape(4 * B, H))).astype(bf16)
    part[...] += mm(gath[...], nw1[H:, :])

    def node_act(i):
        rows = pl.ds(i, CH)
        pre = part[rows, :] + nb1[...]
        g = jax.nn.sigmoid(pre)
        hid[rows, :] = (pre * g).astype(bf16)
        part[rows, :] = g * (1.0 + pre * (1.0 - g))

    unrolled(R, CH, node_act)
    tmp[...] = mm(hid[...], nw2[...])

    def norm(i):
        rows = pl.ds(i, CH)
        o = tmp[rows, :]
        centred = o - jnp.mean(o, axis=1, keepdims=True)
        inv = lax.rsqrt(jnp.mean(centred * centred, axis=1, keepdims=True) + norm_epsilon)
        normed = centred * inv
        fsv[rows, :] = (st[rows, :].astype(f32) + normed * gain[...]).astype(bf16)
        q = ct[rows, :].astype(f32) * gain[...]
        cot = inv * (
            q - jnp.mean(q, axis=1, keepdims=True) - normed * jnp.mean(q * normed, axis=1, keepdims=True)
        )
        cot_out[rows, :] = cot.astype(bf16)

    unrolled(R, CH, norm)
    out_fs = pltpu.make_async_copy(fsv, states_h.at[0], out_sem.at[0])
    out_fs.start()
    tmp[...] = nt(cot_out[...], nw2[...])

    def node_slope(i):
        rows = pl.ds(i, CH)
        cot_pre[rows, :] = (tmp[rows, :] * part[rows, :]).astype(bf16)

    unrolled(R, CH, node_slope)
    cot_g[...] = nt(cot_pre[...], nw1[H:, :]).astype(bf16)

    rets[...] = mm(amat_t[R:, :], cot_g[...]).astype(bf16).reshape(4, B, H)
    home = [
        remote(rets.at[g], ret.at[back[g]], ret_ss.at[g], ret_rs.at[back[g]], sides[g]) for g in range(4)
    ]
    for g in range(4):

        @pl.when(has[g])
        def _():
            home[g].start()

    hn_t[...] = nt(p4[...], hid[...]).astype(bf16)
    g8_t[...] = nt(p8[...], gath[...]).astype(bf16)
    z8, z4 = 2 * K4 * Z, K4 * Z

    def n1_grad(i):
        for y_low, left in ((0, s8_t), (1, g8_t)):
            g = mm(left[pl.ds(i, 2 * z8), :], cot_pre[...])
            sent = jnp.where(first, g[:, HC:], g[:, :HC]).astype(bf16)
            kept = jnp.where(first, g[:, :HC], g[:, HC:])
            for half in range(2):
                q = i // z8 + half
                yy = jnp.where(first, q // 4, q % 2) * 2 + y_low
                xx = jnp.where(first, q % 4, q // 2)
                aa, bb = jnp.where(first, yy, xx), jnp.where(first, xx, yy)
                block = slice(half * z8, (half + 1) * z8)
                n_keep[pl.ds(pl.multiple_of((aa * 4 + bb) * z8, z8), z8), :] = kept[block]
                n_r0s[pl.ds(pl.multiple_of((bb * 4 + aa) * z8, z8), z8), :] = sent[block]

    unrolled(H, 2 * z8, n1_grad)

    def four_rows(base, left, right, keep, send):
        def go(i):
            g = mm(left[pl.ds(i, 4 * z4), :], right[...])
            keep[pl.ds(base + i, 4 * z4), :] = jnp.where(first, g[:, :HC], g[:, HC:])
            sent = jnp.where(first, g[:, HC:], g[:, :HC]).astype(bf16)
            for bb in range(4):
                rows = pl.ds(base + bb * 4 * z4 + i // 4, z4)
                send[rows, :] = sent[bb * z4 : (bb + 1) * z4]

        unrolled(H, 4 * z4, go)

    four_rows(2 * H, hn_t, cot_out, n_keep, n_r0s)
    n_rep = remote(n_r0s, n_r0, n_ss.at[0], n_rs.at[0], partner)
    n_rep.start()
    own[...] = mm(amat_t[:R, :], cot_g[...])
    csp[...] = nt(cot_pre[...], nw1[:H, :])
    s4_t[...] = nt(p4[...], st[...]).astype(bf16)
    for j in range(4):
        for blk in range(BLK):
            fsel[blk * B : (blk + 1) * B, j * B : (j + 1) * B] = jnp.where(
                snd_s[0, j] == blk, eye.astype(f32), 0.0
            ).astype(bf16)

    QC = HC // 2

    def add_partner(parts, keep, got, send):
        def go(i):
            for aa in range(4):
                off = 0
                for base, size in parts:
                    step = size // 4
                    rows = pl.ds(pl.multiple_of(base + aa * size + i * step, step), step)
                    total = (keep[rows, :] + got[rows, :].astype(f32)).astype(bf16)
                    there = pl.ds(pl.multiple_of(off + i * step, step), step)
                    send[0, aa, there, :] = total[:, :QC]
                    send[1, aa, there, :] = total[:, QC:]
                    off += size

        lax.fori_loop(0, 4, lambda i, c: (go(i), c)[1], 0)

    def first_step(send, recv, ss, rs):
        copies = []
        for half, near in ((0, a1), (1, a3)):
            for slot, chunk in ((1, a2), (0, near)):
                k = 1 + 2 * half + slot
                copies.append(
                    remote(send.at[half, chunk], recv.at[half, slot], ss.at[k], rs.at[k], a_at(near))
                )
        for copy in copies:
            copy.start()
        return copies

    def second_step(copies, send, recv, mid_s, mid_r, ss, rs):
        for copy in copies:
            copy.wait_recv()
        more = []
        for half, near in ((0, a3), (1, a1)):
            mid_s[half] = (send[half, near].astype(f32) + recv[half, 1].astype(f32)).astype(bf16)
            k = 5 + half
            copy = remote(mid_s.at[half], mid_r.at[half], ss.at[k], rs.at[k], a_at(near))
            copy.start()
            more.append(copy)
        return more

    def b_stage(copies, send, recv, mid_r, out, got, parts, ss, rs):
        for copy in copies:
            copy.wait_recv()
        for bb in range(4):
            lo = 0
            off = 0
            for size in parts:
                rows = pl.ds(lo + bb * (size // 4), size // 4)
                halves = [
                    send[h, a, rows, :].astype(f32) + recv[h, 0, rows, :].astype(f32) + mid_r[h, rows, :].astype(f32)
                    for h in range(2)
                ]
                out[bb, off : off + size // 4, :] = jnp.concatenate(halves, axis=1).astype(bf16)
                lo += size
                off += size // 4
        more = [
            remote(out.at[(b + j) % 4], got.at[j - 1], ss.at[6 + j], rs.at[6 + j], b_peer(j)) for j in (2, 1, 3)
        ]
        for copy in more:
            copy.start()
        return more

    def b_sum(copies, send, recv):
        for copy in copies:
            copy.wait_recv()
        total = send[b].astype(f32)
        for j in range(3):
            total = total + recv[j].astype(f32)
        return total

    n_parts, e_parts = ((0, 2 * H // 4), (2 * H, H // 4)), ((0, H // 4),)
    n_sizes, e_sizes = (2 * H // 4, H // 4), (H // 4,)
    k8 = 2 * K4

    n_rep.wait_recv()
    add_partner(n_parts, n_keep, n_r0, n_s1s)

    for j in range(4):

        @pl.when(has[j])
        def _():
            home[back[j]].wait_recv()

    n1 = first_step(n_s1s, n_s1, n_ss, n_rs)

    cot_msg[...] = (own[...] + mm(fsel[...], ret[...].reshape(4 * B, H))).astype(bf16)

    four_rows(0, he_t, cot_msg, u_keep, u_r0s)
    u_rep = remote(u_r0s, u_r0, u_ss.at[0], u_rs.at[0], partner)
    u_rep.start()
    tmp[...] = nt(cot_msg[...], ew2[...])

    def edge_slope(i):
        rows = pl.ds(i, CH)
        cot_pre_e[rows, :] = (tmp[rows, :] * slope[rows, :]).astype(bf16)

    unrolled(R, CH, edge_slope)
    four_rows(0, s4_t, cot_pre_e, v_keep, v_r0s)
    v_rep = remote(v_r0s, v_r0, v_ss.at[0], v_rs.at[0], partner)
    v_rep.start()
    u_rep.wait_recv()
    add_partner(e_parts, u_keep, u_r0, u_s1s)
    u1 = first_step(u_s1s, u_s1, u_ss, u_rs)

    csp[...] += nt(cot_pre_e[...], ew1[...])

    def finish_state(i):
        rows = pl.ds(i, CH)
        ct[rows, :] = (ct[rows, :].astype(f32) + csp[rows, :]).astype(bf16)

    unrolled(R, CH, finish_state)
    out_sg = pltpu.make_async_copy(ct, states_h.at[1], out_sem.at[1])
    out_sg.start()

    v_rep.wait_recv()
    add_partner(e_parts, v_keep, v_r0, v_s1s)
    v1 = first_step(v_s1s, v_s1, v_ss, v_rs)
    n2 = second_step(n1, n_s1s, n_s1, n_ts, n_t, n_ss, n_rs)
    u2 = second_step(u1, u_s1s, u_s1, u_ts, u_t, u_ss, u_rs)
    v2 = second_step(v1, v_s1s, v_s1, v_ts, v_t, v_ss, v_rs)
    n3 = b_stage(n2, n_s1s, n_s1, n_t, n_s2s, n_s2, n_sizes, n_ss, n_rs)
    u3 = b_stage(u2, u_s1s, u_s1, u_t, u_s2s, u_s2, e_sizes, u_ss, u_rs)
    v3 = b_stage(v2, v_s1s, v_s1, v_t, v_s2s, v_s2, e_sizes, v_ss, v_rs)

    rows_n = b_sum(n3, n_s2s, n_s2)
    for zz in range(Z):
        pair = z8 + (zz // 2) * k8
        n_s3s[zz] = jnp.concatenate([rows_n[zz * k8 : (zz + 1) * k8], rows_n[pair : pair + k8]], axis=0).astype(bf16)
    n4 = []
    for j in range(1, Z):
        k = 9 + j
        n4.append(remote(n_s3s.at[(z + j) % Z], n_s3.at[j - 1], n_ss.at[k], n_rs.at[k], z_peer(j)))
    for copy in n4:
        copy.start()
    rows_u = b_sum(u3, u_s2s, u_s2)
    rows_v = b_sum(v3, v_s2s, v_s2)
    for zz in range(Z):
        e_s3s[zz] = jnp.concatenate(
            [rows_v[zz * K4 : (zz + 1) * K4], rows_u[zz * K4 : (zz + 1) * K4]], axis=0
        ).astype(bf16)
    e4 = []
    for j in range(1, Z):
        e4.append(remote(e_s3s.at[(z + j) % Z], e_s3.at[0, j], e_ss.at[j], e_rs.at[j], z_peer(j)))
    for j in range(Z):
        e4.append(remote(e_s3s.at[(z + j) % Z], e_s3.at[1, j], e_ss.at[Z + j], e_rs.at[Z + j], across(j)))
    for copy in e4:
        copy.start()

    def whole(mine, theirs):
        return jnp.concatenate([jnp.where(first, mine, theirs), jnp.where(first, theirs, mine)], axis=1)

    for copy in n4:
        copy.wait_recv()
    total = n_s3s[z].astype(f32)
    for j in range(Z - 1):
        total = total + n_s3[j].astype(f32)
    n_fs[...] = total
    n_fin = remote(n_fs, n_f, n_ss.at[9 + Z], n_rs.at[9 + Z], partner)
    n_fin.start()
    n_fin.wait_recv()
    full = whole(n_fs[...], n_f[...])
    grads[:k8, :] = full[:k8]
    grads[k8 : k8 + K4, :] = jnp.where(z % 2 == 1, full[k8 + K4 :], full[k8 : k8 + K4])
    out_fs.wait()
    out_sg.wait()
    for j in range(4):

        @pl.when(has[j])
        def _():
            halo[j].wait_send()
            home[j].wait_send()

    for copy in [n_rep, u_rep, v_rep, n_fin] + n1 + n2 + n3 + n4 + u1 + u2 + u3 + v1 + v2 + v3:
        copy.wait_send()
    for copy in e4:
        copy.wait_recv()
    mine, theirs = e_s3s[z].astype(f32), e_s3[1, 0].astype(f32)
    for j in range(1, Z):
        mine = mine + e_s3[0, j].astype(f32)
        theirs = theirs + e_s3[1, j].astype(f32)
    grads[2 * k8 :, :] = whole(mine, theirs)

    for copy in e4:
        copy.wait_send()


def deliver(K4, states, grads, fs_h, sg_h, ge1_h, ge2_h, gn1_h, gn2_h, ge1, ge2, gn1, gn2, sem):
    out = [pltpu.make_async_copy(states.at[i], ref, sem.at[i]) for i, ref in enumerate((fs_h, sg_h))]
    for copy in out:
        copy.start()
    gn1[...] = grads[: 2 * K4, :]
    gn2[...] = grads[2 * K4 : 3 * K4, :]
    ge1[...] = grads[4 * K4 : 5 * K4, :]
    ge2[...] = grads[5 * K4 :, :]
    for i, (src, dst) in enumerate(((gn1, gn1_h), (gn2, gn2_h), (ge1, ge1_h), (ge2, ge2_h))):
        copy = pltpu.make_async_copy(src, dst, sem.at[2 + i])
        copy.start()
        out.append(copy)
    for copy in out:
        copy.wait()


def make_body(Z, X):
    def body(
        node_state, node_cot, edge_w1, edge_b1, edge_w2, node_w1, node_b1, node_w2, norm_gain,
        tile_dst, tile_src, tile_count, tile_vals, send_blocks,
    ):
        R, H = node_state.shape[3:]
        T, B = tile_vals.shape[2:4]
        Y = Y_LO * Y_HI
        HC = H // 2
        K4 = H // (Z * X * Y)
        k8 = 2 * K4

        def v(shape, dtype=bf16):
            return pltpu.VMEM(shape, dtype)

        def stages(total, s1, s2):
            return [
                v((total, HC), f32), v((total, HC)), v((total, HC)),
                v((2, 4, s1, HC // 2)), v((2, 2, s1, HC // 2)), v((2, s1, HC // 2)), v((2, s1, HC // 2)),
                v((4, s2, HC)), v((3, s2, HC)),
            ]

        dma = pltpu.SemaphoreType.DMA
        scratch = [pltpu.SMEM((1, T), i32), pltpu.SMEM((1, T), i32), pltpu.SMEM((1, 1), i32), pltpu.SMEM((1, 4), i32)]
        scratch += [v((1, H), f32)] * 3
        scratch += [
            v((R, H)), v((R, H)), v((H, H)), v((H, H)), v((2 * H, H)), v((H, H)), v((T, B, B)), dma((14,)),
            v((R, H), f32), v((R, H)), v((BLK, B, H)), v((4, B, H)), v((4, B, H)), v((T, BLK * EXTENT, 16, B)),
            v((R, EXTENT * B)), v((EXTENT * B, R)), v((H, H)), v((H, H)),
            v((H, R)), v((H, R)), v((H, R)), v((H, R)), v((H, R)), v((R, H), f32), v((R, H)), v((R, H)), v((R, H)),
            v((R, H)), v((R, H), f32), v((R, H), f32), v((R, H), f32), v((R, H)),
            v((4, B, H)), v((4, B, H)), v((R, 4 * B)), v((R, H)), v((R, H)),
        ]
        scratch += stages(3 * H, 3 * H // 4, 3 * H // 16)
        scratch += [v((Z, 2 * k8, HC)), v((Z - 1, 2 * k8, HC)), v((2 * k8, HC), f32), v((2 * k8, HC), f32)]
        scratch += stages(H, H // 4, H // 16) * 2
        scratch += [v((Z, k8, HC)), v((2, Z, k8, HC))]
        scratch += [dma((4,))] * 4 + [dma((10 + Z,))] * 2 + [dma((10,))] * 4 + [dma((2 * Z,))] * 2 + [dma((2,))]
        vmem = pl.BlockSpec(memory_space=pltpu.VMEM)
        hbm = pl.BlockSpec(memory_space=pltpu.HBM)
        anywhere = pl.BlockSpec(memory_space=pl.ANY)
        inputs = (
            tile_dst.reshape(1, T), tile_src.reshape(1, T), tile_count, send_blocks.reshape(1, 4),
            edge_b1.reshape(1, H), node_b1.reshape(1, H), norm_gain.reshape(1, H),
            node_state.reshape(R, H), node_cot.reshape(R, H), edge_w1.reshape(H, H), edge_w2.reshape(H, H),
            node_w1.reshape(2 * H, H), node_w2.reshape(H, H), tile_vals.reshape(T, B, B),
        )
        inputs = [
            array if i == 2 else pltpu.with_memory_space_constraint(array, pltpu.HBM) for i, array in enumerate(inputs)
        ]
        states, grads = pl.pallas_call(
            functools.partial(kernel, Z, X, H, B, T),
            out_shape=(jax.ShapeDtypeStruct((2, R, H), bf16), jax.ShapeDtypeStruct((6 * K4, H), f32)),
            in_specs=[hbm] * 14,
            out_specs=(anywhere, vmem),
            scratch_shapes=scratch,
            compiler_params=pltpu.CompilerParams(
                collective_id=0, has_side_effects=True, vmem_limit_bytes=40 * 1024 * 1024
            ),
            name="step",
        )(
            *inputs
        )
        outs = pl.pallas_call(
            functools.partial(deliver, K4),
            out_shape=(
                jax.ShapeDtypeStruct((R, H), bf16),
                jax.ShapeDtypeStruct((R, H), bf16),
                jax.ShapeDtypeStruct((K4, H), f32),
                jax.ShapeDtypeStruct((K4, H), f32),
                jax.ShapeDtypeStruct((k8, H), f32),
                jax.ShapeDtypeStruct((K4, H), f32),
            ),
            in_specs=[anywhere, vmem],
            out_specs=[hbm] * 6,
            scratch_shapes=[v((rows, H), f32) for rows in (K4, K4, k8, K4)] + [dma((6,))],
            compiler_params=pltpu.CompilerParams(vmem_limit_bytes=4 * 1024 * 1024),
            name="deliver",
        )(states, grads)
        return (outs[0].reshape(node_state.shape), outs[1].reshape(node_state.shape)) + tuple(outs[2:])

    return body


def solution(mesh):
    in_specs = (
        P("rep", "stream", "span", None, None),
        P("rep", "stream", "span", None, None),
        P(), P(), P(), P(), P(), P(), P(),
        P("stream", "span", None),
        P("stream", "span", None),
        P("stream", "span"),
        P("stream", "span", None, None, None),
        P("stream", "span", None, None),
    )
    out_specs = (
        P("rep", "stream", "span", None, None),
        P("rep", "stream", "span", None, None),
        P(("stream", "span"), None),
        P(("stream", "span"), None),
        P(("stream", "span"), None),
        P(("stream", "span"), None),
    )
    body = make_body(mesh.shape["stream"] // Y_LO, mesh.shape["span"] // Y_HI)
    return jax.shard_map(body, mesh=mesh, in_specs=in_specs, out_specs=out_specs, check_vma=False)
```
